128 devices in a mesh: row: 8 (over y, z_hi), col: 16 (over x, z_lo, core).
Axes of the slice: x: 4, y: 4, z: 4 (z_hi: 2, z_lo: 2; z = z_hi * 2 + z_lo), core: 2. Of those that a mesh axis runs over, the one named last changes fastest.
Arguments:
- costs: bfloat16 [256, 2048, 128], P('row', 'col'), may hold values from 0 to 63, as said below
- p_small: int32 [1], replicated, may hold values from 4 to 16
- p_large: int32 [1], replicated, may hold values from 32 to 96
Outputs:
- left_view: bfloat16 [256, 2048, 128], P('row', 'col')
- right_view: bfloat16 [256, 2048, 128], P('row', 'col')
The draws below stay inside these ranges and needn't reach their ends.
Inputs may be any that keep to these rules, and one draw needn't show every extreme that they name: `costs`: whole numbers.
All inputs are finite; a program needn't handle non-finite values.
Results may differ from the reference program's by a relative error of at most 0.001.
Values may be sent and summed in bfloat16 or wider, within the bound.
A program may use at most 64 MiB of HBM per device.

```python
import jax
import jax.numpy as jnp
from jax import lax

DISP = 128
TH = 32
TW = 128
H = 256
W = 2048


def draw_costs(key, part):
    keys = jax.random.split(jax.random.fold_in(key, 7), 8)
    span = DISP // 2
    slope_y = jax.random.randint(keys[0], (), 1, 5)
    slope_x = jax.random.randint(keys[1], (), 1, 5)
    offset_base = jax.random.randint(keys[2], (), 0, 8 * span)
    rows = lax.broadcasted_iota(jnp.int32, (H, W), 0)
    cols = lax.broadcasted_iota(jnp.int32, (H, W), 1)
    target = DISP // 4 + (slope_y * rows + slope_x * cols + offset_base) // 8 % span
    levels = lax.broadcasted_iota(jnp.int32, (1, 1, DISP), 2)
    distance = jnp.abs(levels - target[:, :, None])
    noise_top = 24
    flat_share = 3
    noise = jax.random.randint(keys[3], (H, W, DISP), 0, noise_top)
    textured = jnp.minimum(63, noise + jnp.minimum(48, 4 * distance))
    block_rows = 3 * TH
    block_cols = 3 * TW
    offset_rows = jax.random.randint(keys[4], (), 0, block_rows)
    offset_cols = jax.random.randint(keys[5], (), 0, block_cols)
    flags = jax.random.randint(keys[6], ((H + block_rows) // block_rows + 1, (W + block_cols) // block_cols + 1), 0, 6)
    flat_mask = flags[(rows + offset_rows) // block_rows, (cols + offset_cols) // block_cols] < flat_share
    flat_level = jax.random.randint(keys[7], (H, W), 4, 60)
    values = jnp.where(flat_mask[:, :, None], flat_level[:, :, None], textured)
    return values.astype(jnp.float32).astype(jnp.bfloat16)


def setup_inputs(seed: int = 0) -> dict:
    key_list = jax.random.split(jax.random.key(seed), 4)
    costs = draw_costs(jax.random.fold_in(key_list[3], 71), 0)
    p_small = jax.random.randint(key_list[1], (1,), 4, 17).astype(jnp.int32)
    p_large = jax.random.randint(key_list[2], (1,), 32, 97).astype(jnp.int32)
    return dict(costs=costs, p_small=p_small, p_large=p_large)


def advance(before, here_cost, p_one, p_two):
    lowest = jnp.min(before, axis=-1, keepdims=True)
    barrier = jnp.full(before.shape[:-1] + (1,), jnp.inf, before.dtype)
    lower_side = jnp.concatenate([barrier, before[..., :-1]], axis=-1)
    upper_side = jnp.concatenate([before[..., 1:], barrier], axis=-1)
    smallest = jnp.minimum(jnp.minimum(before, jnp.minimum(lower_side, upper_side) + p_one), lowest + p_two)
    return here_cost + smallest - lowest


def one_path(cost_grid, axis_dim, backward, p_one, p_two):
    moved = jnp.moveaxis(cost_grid, axis_dim, 0)

    def advance_one(before, here_cost):
        after = advance(before, here_cost, p_one, p_two)
        return after, after

    _, values = lax.scan(advance_one, jnp.zeros_like(moved[0]), moved, reverse=backward)
    return jnp.moveaxis(values, 0, axis_dim)


def diagonal_view(joined, out_width):
    row_count, span_count, depth = joined.shape
    turned = jnp.transpose(joined, (0, 2, 1)).reshape(row_count, depth * span_count)
    padded = jnp.pad(turned, ((0, 0), (0, depth)))
    sheared = padded.reshape(row_count, depth, span_count + 1)[:, :, :out_width]
    return jnp.transpose(sheared, (0, 2, 1))


def reference(costs, p_small, p_large):
    cost_grid = costs.astype(jnp.float32)
    p_one = p_small[0].astype(jnp.float32)
    p_two = p_large[0].astype(jnp.float32)
    summed = one_path(cost_grid, 1, False, p_one, p_two)
    summed = summed + one_path(cost_grid, 1, True, p_one, p_two)
    summed = summed + one_path(cost_grid, 0, False, p_one, p_two)
    summed = summed + one_path(cost_grid, 0, True, p_one, p_two)
    left_view = (summed * (1.0 / 64.0)).astype(jnp.bfloat16)
    joined = jnp.pad(left_view, ((0, 0), (0, DISP), (0, 0)))
    right_view = diagonal_view(joined, W)
    return left_view, right_view
```

```python
import jax
import jax.numpy as jnp
from jax import lax
from jax.experimental import pallas as pl
from jax.experimental.pallas import tpu as pltpu
from jax.sharding import PartitionSpec as P

MESH = pl.DeviceIdType.MESH
F32 = jnp.float32
BF16 = jnp.bfloat16
FAR = 1.0e9

TH, TW, D = 32, 128, 128
NJ = 16


def nt_dot(a, b):
    return lax.dot_general(a, b, (((1,), (1,)), ((), ())), preferred_element_type=F32)


def to_slab(ref, base, v):
    for a in range(NJ):
        ref[pl.ds(base + (a % 2) * 64 + a // 2, 8, stride=8), :] = v[8 * a : 8 * a + 8]


def from_slab(ref, base):
    return [ref[pl.ds(base + (a % 2) * 64 + a // 2, 8, stride=8), :] for a in range(NJ)]


def step(u, c, q1, q2, first, last):
    low = jnp.where(first, FAR, pltpu.roll(u[NJ - 1], 1, 0))
    high = jnp.where(last, FAR, pltpu.roll(u[0], 7, 0))
    sides = []
    for j in range(NJ):
        a = u[j - 1] if j else low
        b = u[j + 1] if j < NJ - 1 else high
        sides.append(jnp.minimum(a, b))
    parts = [sides[j] for j in range(NJ) if j % 4 in (1, 2)]
    while len(parts) > 1:
        parts = [jnp.minimum(parts[i], parts[i + 1]) for i in range(0, len(parts), 2)]
    m = parts[0]
    for s in (4, 2, 1):
        m = jnp.minimum(m, pltpu.roll(m, s, 0))
    jump = m + q2
    out = [
        jnp.minimum(jnp.minimum(u[j], sides[j] + q1), jump) + c[8 * j : 8 * j + 8]
        for j in range(NJ)
    ]
    return out, m


def kernel(
    small_ref, large_ref, costs_ref, left_ref, right_ref,
    c_h, c_v, path_h, low_h, path_v, low_v, acc, beyond,
    out_h, in_h, out_v, in_v, send_h, recv_h, send_v, recv_v, send_b, recv_b,
):
    row, col = lax.axis_index("row"), lax.axis_index("col")
    rows, cols = lax.axis_size("row"), lax.axis_size("col")

    barrier = pltpu.get_barrier_semaphore()
    partners = [
        (col > 0, row, col - 1),
        (col < cols - 1, row, col + 1),
        (row > 0, row - 1, col),
        (row < rows - 1, row + 1, col),
    ]
    for there, r, c in partners:

        @pl.when(there)
        def _(r=r, c=c):
            pl.semaphore_signal(barrier, inc=1, device_id=(r, c), device_id_type=MESH)

    missing = sum(jnp.where(there, 0, 1) for there, _, _ in partners)
    pl.semaphore_wait(barrier, 4 - missing)

    q1 = jnp.full((8, 128), small_ref[0].astype(F32))
    q2 = jnp.full((8, 128), large_ref[0].astype(F32))
    sub = lax.broadcasted_iota(jnp.int32, (8, 128), 0)
    lane = lax.broadcasted_iota(jnp.int32, (8, 128), 1)
    first, last = sub == 0, sub == 7
    r0 = lax.broadcasted_iota(jnp.int32, (D, D), 0)
    r1 = lax.broadcasted_iota(jnp.int32, (D, D), 1)
    perm = (r1 == (r0 % 8) * 16 + r0 // 8).astype(F32).astype(BF16)

    @pl.loop(0, TH)
    def _(y):
        acc[pl.ds(pl.multiple_of(y * TW, TW), TW), :] = costs_ref[y].astype(F32)

    @pl.loop(0, TW // 4)
    def _(g):
        for k in range(4):
            x = 4 * g + k
            a = acc[pl.ds(x, TH, stride=TW), :]
            if k % 2:
                a = a.astype(BF16)
                c_h[pl.ds(pl.multiple_of(x * D, D), D), :] = nt_dot(perm, jnp.concatenate([a] * 4, axis=0))
            else:
                to_slab(c_h, x * D, jnp.transpose(jnp.concatenate([a] * 4, axis=0)))

    def columns():
        @pl.loop(0, TH, unroll=4)
        def _(y):
            c_v[pl.ds(pl.multiple_of(y * D, D), D), :] = nt_dot(perm, costs_ref[y])

    def h_copy(way):
        return pltpu.make_async_remote_copy(
            out_h.at[way], in_h.at[way], send_h.at[way], recv_h.at[way],
            device_id=(row, col + 1 - 2 * way), device_id_type=MESH,
        )

    def v_copy(way):
        return pltpu.make_async_remote_copy(
            out_v.at[way], in_v.at[way], send_v.at[way], recv_v.at[way],
            device_id=(row + 1 - 2 * way, col), device_id_type=MESH,
        )

    def along_row(way):
        at = jnp.where(way == 0, col, cols - 1 - col)

        @pl.when(at == 0)
        def _():
            in_h[way] = jnp.zeros((32, 128), BF16)

        @pl.when(at > 0)
        def _():
            h_copy(way).wait_recv()

        got = in_h[way].astype(F32)
        got = [got[8 * i : 8 * i + 8] for i in range(4)]
        turned = [[v] + [pltpu.roll(v, 32 * k, 1) for k in (1, 2, 3)] for v in got]
        u = []
        for g in range(4):
            for i in range(4):
                v = turned[i][-g % 4]
                for h in range(1, 4):
                    v = jnp.where(lane >= 32 * h, turned[i][(h - g) % 4], v)
                u.append(v)

        def body(t, carry):
            u, _ = carry
            x = jnp.where(way == 0, t, TW - 1 - t)
            at = pl.ds(pl.multiple_of(x * D, D), D)
            u, m = step(u, c_h[at, :], q1, q2, first, last)
            mine = lane // 32 == x % 4
            base = pl.multiple_of(x // 4 * D, D)
            for j in range(NJ):
                pltpu.store(path_h.at[way, pl.ds(base + 8 * j, 8), :], u[j], mask=mine)
            pltpu.store(low_h.at[way, x // 4], m, mask=mine)
            return u, m

        u, m = lax.fori_loop(0, TW, body, (u, jnp.zeros((8, 128), F32)), unroll=4)

        @pl.when(at < cols - 1)
        def _():
            packed = []
            for i in range(4):
                v = u[i]
                for g in range(1, 4):
                    v = jnp.where(lane >= 32 * g, u[4 * g + i], v)
                packed.append(v - m)
            out_h[way] = jnp.concatenate(packed, axis=0).astype(BF16)
            h_copy(way).start()

    def along_col(way):
        at = jnp.where(way == 0, row, rows - 1 - row)

        @pl.when(at == 0)
        def _():
            in_v[way] = jnp.zeros((D, 128), BF16)

        @pl.when(at > 0)
        def _():
            v_copy(way).wait_recv()

        got = in_v[way].astype(F32)
        u = [got[8 * j : 8 * j + 8] for j in range(NJ)]

        def body(t, carry):
            u, _ = carry
            y = jnp.where(way == 0, t, TH - 1 - t)
            at = pl.ds(pl.multiple_of(y * D, D), D)
            u, m = step(u, c_v[at, :], q1, q2, first, last)
            path_v[way, at, :] = jnp.concatenate(u, axis=0)
            low_v[way, y] = m
            return u, m

        u, m = lax.fori_loop(0, TH, body, (u, jnp.zeros((8, 128), F32)), unroll=2)

        @pl.when(at < rows - 1)
        def _():
            out_v[way] = jnp.concatenate([v - m for v in u], axis=0).astype(BF16)
            v_copy(way).start()

    near = jnp.minimum(col, cols - 1 - col)
    h_one = jnp.where(col * 2 < cols, 0, 1)
    v_near = jnp.minimum(row, rows - 1 - row)
    v_one = jnp.where(row * 2 < rows, 0, 1)
    before = (near * 3) // 4
    until = before + ((cols - 2 - 2 * near) * 3) // 4

    def add_columns():
        @pl.loop(0, TH, unroll=2)
        def _(y):
            base = pl.multiple_of(y * D, D)
            low = low_v[0, y] + low_v[1, y]
            both = zip(from_slab(path_v.at[0], base), from_slab(path_v.at[1], base))
            acc[pl.ds(base, TW), :] = jnp.transpose(jnp.concatenate([a + b - low for a, b in both], axis=0))

    def add_rows(way):
        @pl.loop(0, TW // 4, unroll=2)
        def _(g):
            low = low_h[way, g]
            v = [a - low for a in from_slab(path_h.at[way], pl.multiple_of(g * D, D))]
            v = jnp.transpose(jnp.concatenate(v, axis=0))
            for k in range(4):
                at = pl.ds(4 * g + k, TH, stride=TW)
                acc[at, :] = acc[at, :] + v[TH * k : TH * (k + 1)]

    v_late = rows - 1 - v_near >= until

    @pl.loop(0, 9)
    def _(p):
        part, which = p // 3, p % 3
        slot = jnp.where(which == 0, v_near, rows - 1 - v_near)
        v_part = jnp.where(slot < before, 0, jnp.where(slot < until, 1, 2))

        @pl.when(p == jnp.where(near < 2, 3, 0))
        def _():
            columns()

        @pl.when(p == jnp.where(v_late, 8, 5))
        def _():
            add_columns()
            add_rows(h_one)

        @pl.when(jnp.logical_and(which == 2, part < 2))
        def _():
            along_row(jnp.where(part == 0, h_one, 1 - h_one))

        @pl.when(jnp.logical_and(which < 2, v_part == part))
        def _():
            along_col(jnp.where(which == 0, v_one, 1 - v_one))

    add_rows(1 - h_one)

    CH = TH // 4

    def next_tile(q):
        at = pl.ds(q * CH, CH)
        return pltpu.make_async_remote_copy(
            left_ref.at[at], beyond.at[at], send_b.at[q], recv_b.at[q],
            device_id=(row, col - 1), device_id_type=MESH,
        )

    @pl.loop(0, 4)
    def _(q):
        @pl.loop(q * CH, (q + 1) * CH)
        def _(y):
            left_ref[y] = (acc[pl.ds(pl.multiple_of(y * TW, TW), TW), :] * (1.0 / 64.0)).astype(BF16)

        @pl.when(col > 0)
        def _():
            next_tile(q).start()

    @pl.when(col == cols - 1)
    def _():
        beyond[...] = jnp.zeros((TH, TW, D), BF16)

    @pl.loop(0, 4)
    def _(q):
        @pl.when(col < cols - 1)
        def _():
            next_tile(q).wait_recv()

        @pl.loop(q * CH, (q + 1) * CH)
        def _(y):
            v = jnp.concatenate([left_ref[y], beyond[y]], axis=0).astype(F32)
            for bit, size in ((64, 192), (32, 160), (16, 144), (8, 136)):
                d = lax.broadcasted_iota(jnp.int32, (size, D), 1)
                v = jnp.where((d & bit) != 0, v[bit : bit + size], v[:size])
            d = lax.broadcasted_iota(jnp.int32, (136, D), 1)
            for bit in (4, 2, 1):
                v = jnp.where((d & bit) != 0, pltpu.roll(v, 136 - bit, 0), v)
            right_ref[y] = v[:TW].astype(BF16)

    for way in (0, 1):
        at_h = col if way == 0 else cols - 1 - col
        at_v = row if way == 0 else rows - 1 - row

        @pl.when(at_h < cols - 1)
        def _(way=way):
            h_copy(way).wait_send()

        @pl.when(at_v < rows - 1)
        def _(way=way):
            v_copy(way).wait_send()

    @pl.when(col > 0)
    def _():
        for q in range(4):
            next_tile(q).wait_send()


def shards(costs, p_small, p_large):
    tile = jax.ShapeDtypeStruct(costs.shape, BF16)
    return pl.pallas_call(
        kernel,
        out_shape=(tile, tile),
        in_specs=[
            pl.BlockSpec(memory_space=pltpu.SMEM),
            pl.BlockSpec(memory_space=pltpu.SMEM),
            pl.BlockSpec(memory_space=pltpu.VMEM),
        ],
        out_specs=(pl.BlockSpec(memory_space=pltpu.VMEM), pl.BlockSpec(memory_space=pltpu.VMEM)),
        scratch_shapes=[
            pltpu.VMEM((TW * D, 128), F32),
            pltpu.VMEM((TH * D, 128), F32),
            pltpu.VMEM((2, TW // 4 * D, 128), F32),
            pltpu.VMEM((2, TW // 4, 8, 128), F32),
            pltpu.VMEM((2, TH * D, 128), F32),
            pltpu.VMEM((2, TH, 8, 128), F32),
            pltpu.VMEM((TH * TW, D), F32),
            pltpu.VMEM((TH, TW, D), BF16),
            pltpu.VMEM((2, 32, 128), BF16),
            pltpu.VMEM((2, 32, 128), BF16),
            pltpu.VMEM((2, D, 128), BF16),
            pltpu.VMEM((2, D, 128), BF16),
            pltpu.SemaphoreType.DMA((2,)),
            pltpu.SemaphoreType.DMA((2,)),
            pltpu.SemaphoreType.DMA((2,)),
            pltpu.SemaphoreType.DMA((2,)),
            pltpu.SemaphoreType.DMA((4,)),
            pltpu.SemaphoreType.DMA((4,)),
        ],
        compiler_params=pltpu.CompilerParams(collective_id=0, has_side_effects=True),
        name="sgm",
    )(p_small, p_large, costs)


def solution(mesh):
    placed = (P("row", "col", None), P(), P())
    return jax.shard_map(
        shards,
        mesh=mesh,
        in_specs=placed,
        out_specs=(P("row", "col", None), P("row", "col", None)),
        check_vma=False,
    )
```

```python
import jax
import jax.numpy as jnp
from jax import lax
from jax.experimental import pallas as pl
from jax.experimental.pallas import tpu as pltpu
from jax.sharding import PartitionSpec as P

MESH = pl.DeviceIdType.MESH
F32 = jnp.float32
BF16 = jnp.bfloat16
FAR = 1.0e9

TH, TW, D = 32, 128, 128
NJ = 16
FOLD = 80
PITCH = 136


def nt_dot(a, b):
    return lax.dot_general(a, b, (((1,), (1,)), ((), ())), preferred_element_type=F32)


def to_slab(ref, base, v):
    for a in range(NJ):
        ref[pl.ds(base + (a % 2) * 64 + a // 2, 8, stride=8), :] = v[8 * a : 8 * a + 8]


def from_slab(ref, base):
    return [ref[pl.ds(base + (a % 2) * 64 + a // 2, 8, stride=8), :] for a in range(NJ)]


def step(u, c, q1, q2, first, last):
    low = jnp.where(first, FAR, pltpu.roll(u[NJ - 1], 1, 0))
    high = jnp.where(last, FAR, pltpu.roll(u[0], 7, 0))
    sides = []
    for j in range(NJ):
        a = u[j - 1] if j else low
        b = u[j + 1] if j < NJ - 1 else high
        sides.append(jnp.minimum(a, b))
    parts = [sides[j] for j in range(NJ) if j % 4 in (1, 2)]
    while len(parts) > 1:
        parts = [jnp.minimum(parts[i], parts[i + 1]) for i in range(0, len(parts), 2)]
    m = parts[0]
    for s in (4, 2, 1):
        m = jnp.minimum(m, pltpu.roll(m, s, 0))
    jump = m + q2
    out = [
        jnp.minimum(jnp.minimum(u[j], sides[j] + q1), jump) + c[8 * j : 8 * j + 8]
        for j in range(NJ)
    ]
    return out, m


def kernel(
    small_ref, large_ref, costs_ref, left_out, right_out, left_ref, right_ref, folded,
    c_h, c_v, path_h, low_h, path_v, low_v, acc, beyond,
    out_h, in_h, out_v, in_v, send_h, recv_h, send_v, recv_v, send_b, recv_b, done_l, done_r,
):
    row, col = lax.axis_index("row"), lax.axis_index("col")
    rows, cols = lax.axis_size("row"), lax.axis_size("col")

    barrier = pltpu.get_barrier_semaphore()
    partners = [
        (col > 0, row, col - 1),
        (col < cols - 1, row, col + 1),
        (row > 0, row - 1, col),
        (row < rows - 1, row + 1, col),
    ]
    for there, r, c in partners:

        @pl.when(there)
        def _(r=r, c=c):
            pl.semaphore_signal(barrier, inc=1, device_id=(r, c), device_id_type=MESH)

    missing = sum(jnp.where(there, 0, 1) for there, _, _ in partners)
    pl.semaphore_wait(barrier, 4 - missing)

    q1 = jnp.full((8, 128), small_ref[0].astype(F32))
    q2 = jnp.full((8, 128), large_ref[0].astype(F32))
    sub = lax.broadcasted_iota(jnp.int32, (8, 128), 0)
    lane = lax.broadcasted_iota(jnp.int32, (8, 128), 1)
    first, last = sub == 0, sub == 7
    r0 = lax.broadcasted_iota(jnp.int32, (D, D), 0)
    r1 = lax.broadcasted_iota(jnp.int32, (D, D), 1)
    perm = (r1 == (r0 % 8) * 16 + r0 // 8).astype(F32).astype(BF16)

    @pl.loop(0, TH)
    def _(y):
        acc[pl.ds(pl.multiple_of(y * PITCH, 8), TW), :] = costs_ref[y].astype(F32)

    @pl.loop(0, TW // 4)
    def _(g):
        for k in range(4):
            x = 4 * g + k
            a = acc[pl.ds(x, TH, stride=PITCH), :]
            if k % 2:
                a = a.astype(BF16)
                c_h[pl.ds(pl.multiple_of(x * D, D), D), :] = nt_dot(perm, jnp.concatenate([a] * 4, axis=0))
            else:
                to_slab(c_h, x * D, jnp.transpose(jnp.concatenate([a] * 4, axis=0)))

    def columns():
        @pl.loop(0, TH, unroll=4)
        def _(y):
            c_v[pl.ds(pl.multiple_of(y * D, D), D), :] = nt_dot(perm, costs_ref[y])

    def h_copy(way):
        return pltpu.make_async_remote_copy(
            out_h.at[way], in_h.at[way], send_h.at[way], recv_h.at[way],
            device_id=(row, col + 1 - 2 * way), device_id_type=MESH,
        )

    def v_copy(way):
        return pltpu.make_async_remote_copy(
            out_v.at[way], in_v.at[way], send_v.at[way], recv_v.at[way],
            device_id=(row + 1 - 2 * way, col), device_id_type=MESH,
        )

    def along_row(way):
        at = jnp.where(way == 0, col, cols - 1 - col)

        @pl.when(at == 0)
        def _():
            in_h[way] = jnp.zeros((32, 128), BF16)

        @pl.when(at > 0)
        def _():
            h_copy(way).wait_recv()

        got = in_h[way].astype(F32)
        got = [got[8 * i : 8 * i + 8] for i in range(4)]
        turned = [[v] + [pltpu.roll(v, 32 * k, 1) for k in (1, 2, 3)] for v in got]
        u = []
        for g in range(4):
            for i in range(4):
                v = turned[i][-g % 4]
                for h in range(1, 4):
                    v = jnp.where(lane >= 32 * h, turned[i][(h - g) % 4], v)
                u.append(v)

        def body(t, carry):
            u, _ = carry
            x = jnp.where(way == 0, t, TW - 1 - t)
            at = pl.ds(pl.multiple_of(x * D, D), D)
            u, m = step(u, c_h[at, :], q1, q2, first, last)
            mine = lane // 32 == x % 4
            base = pl.multiple_of(x // 4 * D, D)
            for j in range(NJ):
                pltpu.store(path_h.at[way, pl.ds(base + 8 * j, 8), :], u[j], mask=mine)
            pltpu.store(low_h.at[way, x // 4], m, mask=mine)
            return u, m

        u, m = lax.fori_loop(0, TW, body, (u, jnp.zeros((8, 128), F32)), unroll=4)

        @pl.when(at < cols - 1)
        def _():
            packed = []
            for i in range(4):
                v = u[i]
                for g in range(1, 4):
                    v = jnp.where(lane >= 32 * g, u[4 * g + i], v)
                packed.append(v - m)
            out_h[way] = jnp.concatenate(packed, axis=0).astype(BF16)
            h_copy(way).start()

    def along_col(way):
        at = jnp.where(way == 0, row, rows - 1 - row)

        @pl.when(at == 0)
        def _():
            in_v[way] = jnp.zeros((D, 128), BF16)

        @pl.when(at > 0)
        def _():
            v_copy(way).wait_recv()

        got = in_v[way].astype(F32)
        u = [got[8 * j : 8 * j + 8] for j in range(NJ)]

        def body(t, carry):
            u, _ = carry
            y = jnp.where(way == 0, t, TH - 1 - t)
            at = pl.ds(pl.multiple_of(y * D, D), D)
            u, m = step(u, c_v[at, :], q1, q2, first, last)
            path_v[way, at, :] = jnp.concatenate(u, axis=0)
            low_v[way, y] = m
            return u, m

        u, m = lax.fori_loop(0, TH, body, (u, jnp.zeros((8, 128), F32)), unroll=2)

        @pl.when(at < rows - 1)
        def _():
            out_v[way] = jnp.concatenate([v - m for v in u], axis=0).astype(BF16)
            v_copy(way).start()

    near = jnp.minimum(col, cols - 1 - col)
    h_one = jnp.where(col * 2 < cols, 0, 1)
    v_near = jnp.minimum(row, rows - 1 - row)
    v_one = jnp.where(row * 2 < rows, 0, 1)
    before = (near * 3) // 4
    until = before + ((cols - 2 - 2 * near) * 3) // 4

    def add_columns():
        @pl.loop(0, TH, unroll=2)
        def _(y):
            base = pl.multiple_of(y * D, D)
            low = low_v[0, y] + low_v[1, y]
            both = zip(from_slab(path_v.at[0], base), from_slab(path_v.at[1], base))
            acc[pl.ds(pl.multiple_of(y * PITCH, 8), TW), :] = jnp.transpose(jnp.concatenate([a + b - low for a, b in both], axis=0))

    def add_rows(way):
        @pl.loop(0, TW // 4, unroll=2)
        def _(g):
            low = low_h[way, g]
            v = [a - low for a in from_slab(path_h.at[way], pl.multiple_of(g * D, D))]
            v = jnp.transpose(jnp.concatenate(v, axis=0))
            for k in range(4):
                at = pl.ds(4 * g + k, TH, stride=PITCH)
                acc[at, :] = acc[at, :] + v[TH * k : TH * (k + 1)]

    v_late = rows - 1 - v_near >= until

    @pl.loop(0, 9)
    def _(p):
        part, which = p // 3, p % 3
        slot = jnp.where(which == 0, v_near, rows - 1 - v_near)
        v_part = jnp.where(slot < before, 0, jnp.where(slot < until, 1, 2))

        @pl.when(p == jnp.where(near < 2, 3, 0))
        def _():
            columns()

        @pl.when(p == jnp.where(v_late, 8, 5))
        def _():
            add_columns()
            add_rows(h_one)

        @pl.when(jnp.logical_and(which == 2, part < 2))
        def _():
            along_row(jnp.where(part == 0, h_one, 1 - h_one))

        @pl.when(jnp.logical_and(which < 2, v_part == part))
        def _():
            along_col(jnp.where(which == 0, v_one, 1 - v_one))

    add_rows(1 - h_one)

    CH = TH // 4

    def next_tile(q):
        at = pl.ds(q * CH, CH)
        return pltpu.make_async_remote_copy(
            folded.at[at], beyond.at[at], send_b.at[q], recv_b.at[q],
            device_id=(row, col - 1), device_id_type=MESH,
        )

    def write(src, dst, sem, q):
        at = pl.ds(q * CH, CH)
        return pltpu.make_async_copy(src.at[at], dst.at[at], sem.at[q])

    lane32 = lax.broadcasted_iota(jnp.int32, (32, D), 1)

    @pl.loop(0, 4)
    def _(q):
        @pl.loop(q * CH, (q + 1) * CH)
        def _(y):
            v = acc[pl.ds(pl.multiple_of(y * PITCH, 8), TW), :] * (1.0 / 64.0)
            left_ref[y] = v.astype(BF16)
            one = jnp.where(lane32 < 32, pltpu.roll(v[96:], 32, 1), v[32:64])
            two = jnp.where(lane32[:16] < 64, pltpu.roll(v[80:96], 64, 1), v[64:80])
            folded[y] = jnp.concatenate([v[:32], one, two], axis=0).astype(BF16)

        @pl.when(col > 0)
        def _():
            next_tile(q).start()

        write(left_ref, left_out, done_l, q).start()

    @pl.when(col == cols - 1)
    def _():
        beyond[...] = jnp.zeros((TH, FOLD, D), BF16)

    @pl.loop(0, 4)
    def _(q):
        @pl.when(col < cols - 1)
        def _():
            next_tile(q).wait_recv()

        @pl.loop(q * CH, (q + 1) * CH)
        def _(y):
            f = beyond[y].astype(F32)
            v = jnp.concatenate(
                [left_ref[y].astype(F32), f, pltpu.roll(f[64:80], 64, 1), pltpu.roll(f[32:64], 96, 1)], axis=0
            )
            for bit, size in ((64, 192), (32, 160), (16, 144), (8, 136)):
                d = lax.broadcasted_iota(jnp.int32, (size, D), 1)
                v = jnp.where((d & bit) != 0, v[bit : bit + size], v[:size])
            d = lax.broadcasted_iota(jnp.int32, (136, D), 1)
            for bit in (4, 2, 1):
                v = jnp.where((d & bit) != 0, pltpu.roll(v, 136 - bit, 0), v)
            right_ref[y] = v[:TW].astype(BF16)

        write(right_ref, right_out, done_r, q).start()

    for q in range(4):
        write(left_ref, left_out, done_l, q).wait()
        write(right_ref, right_out, done_r, q).wait()

    for way in (0, 1):
        at_h = col if way == 0 else cols - 1 - col
        at_v = row if way == 0 else rows - 1 - row

        @pl.when(at_h < cols - 1)
        def _(way=way):
            h_copy(way).wait_send()

        @pl.when(at_v < rows - 1)
        def _(way=way):
            v_copy(way).wait_send()

    @pl.when(col > 0)
    def _():
        for q in range(4):
            next_tile(q).wait_send()


def shards(costs, p_small, p_large):
    tile = jax.ShapeDtypeStruct(costs.shape, BF16)
    return pl.pallas_call(
        kernel,
        out_shape=(tile, tile),
        in_specs=[
            pl.BlockSpec(memory_space=pltpu.SMEM),
            pl.BlockSpec(memory_space=pltpu.SMEM),
            pl.BlockSpec(memory_space=pltpu.VMEM),
        ],
        out_specs=(pl.BlockSpec(memory_space=pl.ANY), pl.BlockSpec(memory_space=pl.ANY)),
        scratch_shapes=[
            pltpu.VMEM((TH, TW, D), BF16),
            pltpu.VMEM((TH, TW, D), BF16),
            pltpu.VMEM((TH, FOLD, D), BF16),
            pltpu.VMEM((TW * D, 128), F32),
            pltpu.VMEM((TH * D, 128), F32),
            pltpu.VMEM((2, TW // 4 * D, 128), F32),
            pltpu.VMEM((2, TW // 4, 8, 128), F32),
            pltpu.VMEM((2, TH * D, 128), F32),
            pltpu.VMEM((2, TH, 8, 128), F32),
            pltpu.VMEM((TH * PITCH, D), F32),
            pltpu.VMEM((TH, FOLD, D), BF16),
            pltpu.VMEM((2, 32, 128), BF16),
            pltpu.VMEM((2, 32, 128), BF16),
            pltpu.VMEM((2, D, 128), BF16),
            pltpu.VMEM((2, D, 128), BF16),
            pltpu.SemaphoreType.DMA((2,)),
            pltpu.SemaphoreType.DMA((2,)),
            pltpu.SemaphoreType.DMA((2,)),
            pltpu.SemaphoreType.DMA((2,)),
            pltpu.SemaphoreType.DMA((4,)),
            pltpu.SemaphoreType.DMA((4,)),
            pltpu.SemaphoreType.DMA((4,)),
            pltpu.SemaphoreType.DMA((4,)),
        ],
        compiler_params=pltpu.CompilerParams(collective_id=0, has_side_effects=True),
        name="sgm",
    )(p_small, p_large, costs)


def solution(mesh):
    placed = (P("row", "col", None), P(), P())
    return jax.shard_map(
        shards,
        mesh=mesh,
        in_specs=placed,
        out_specs=(P("row", "col", None), P("row", "col", None)),
        check_vma=False,
    )
```

```python
import jax
import jax.numpy as jnp
from jax import lax
from jax.experimental import pallas as pl
from jax.experimental.pallas import tpu as pltpu
from jax.sharding import PartitionSpec as P

MESH = pl.DeviceIdType.MESH
F32 = jnp.float32
BF16 = jnp.bfloat16
FAR = 1.0e9

TH, TW, D = 32, 128, 128
NJ = 8
FOLD = 80
PITCH = 136


def nt_dot(a, b):
    return lax.dot_general(a, b, (((1,), (1,)), ((), ())), preferred_element_type=F32)


def nn_dot(a, b):
    return lax.dot_general(a, b, (((1,), (0,)), ((), ())), preferred_element_type=F32)


def registers(slab):
    return [slab[16 * j : 16 * j + 16] for j in range(NJ)]


def least(parts):
    parts = list(parts)
    while len(parts) > 1:
        parts = [jnp.minimum(parts[i], parts[i + 1]) for i in range(0, len(parts), 2)]
    m = parts[0].astype(F32)
    m = jnp.minimum(m[:8], m[8:])
    for s in (4, 2, 1):
        m = jnp.minimum(m, pltpu.roll(m, s, 0))
    return m


def step(v, m, c, cq, cm, q1, q1_low, q1_high):
    low = pltpu.roll(v[NJ - 1], 1, 0) + q1_low
    high = pltpu.roll(v[0], 15, 0) + q1_high
    w = []
    for j in range(NJ):
        if j == 0:
            sides = jnp.minimum(low, v[1] + q1)
        elif j == NJ - 1:
            sides = jnp.minimum(high, v[NJ - 2] + q1)
        else:
            sides = jnp.minimum(v[j - 1], v[j + 1]) + q1
        w.append(jnp.minimum(v[j], sides) + c[j])
    a = least([w[1], w[2], w[3], w[4], w[5], w[6], w[0], w[7]])
    whole = jnp.concatenate([m, m], axis=0).astype(BF16)
    return [jnp.minimum(w[j] - whole, cq[j]) for j in range(NJ)], jnp.minimum(a - m, cm)


def kernel(
    small_ref, large_ref, costs_ref, left_out, right_out, left_ref, right_ref, folded,
    c_h, cq_h, cm_h, c_v, cq_v, cm_v, path_h, path_v, acc, beyond,
    out_h, in_h, out_v, in_v, send_h, recv_h, send_v, recv_v, send_b, recv_b, done_l, done_r,
):
    row, col = lax.axis_index("row"), lax.axis_index("col")
    rows, cols = lax.axis_size("row"), lax.axis_size("col")

    barrier = pltpu.get_barrier_semaphore()
    partners = [
        (col > 0, row, col - 1),
        (col < cols - 1, row, col + 1),
        (row > 0, row - 1, col),
        (row < rows - 1, row + 1, col),
    ]
    for there, r, c in partners:

        @pl.when(there)
        def _(r=r, c=c):
            pl.semaphore_signal(barrier, inc=1, device_id=(r, c), device_id_type=MESH)


    q1f = jnp.full((16, 128), small_ref[0].astype(F32))
    q2f = jnp.full((16, 128), large_ref[0].astype(F32))
    sub = lax.broadcasted_iota(jnp.int32, (16, 128), 0)
    q1, q2 = q1f.astype(BF16), q2f.astype(BF16)
    q1_low = jnp.where(sub == 0, FAR, q1f).astype(BF16)
    q1_high = jnp.where(sub == 15, FAR, q1f).astype(BF16)
    lane = lax.broadcasted_iota(jnp.int32, (16, 128), 1)
    after = [lane >= 32 * h for h in range(4)]
    r0 = lax.broadcasted_iota(jnp.int32, (D, D), 0)
    r1 = lax.broadcasted_iota(jnp.int32, (D, D), 1)
    perm = (r1 == (r0 % 16) * 8 + r0 // 16).astype(F32).astype(BF16)
    back = (r0 == (r1 % 16) * 8 + r1 // 16).astype(F32).astype(BF16)

    def keep(c_ref, cq_ref, cm_ref, n, slab):
        slab = slab.astype(BF16)
        cq = [c + q2 for c in registers(slab)]
        c_ref[n] = slab
        cq_ref[n] = jnp.concatenate(cq, axis=0)
        cm_ref[n] = least(cq)

    @pl.loop(0, TH)
    def _(y):
        acc[pl.ds(pl.multiple_of(y * PITCH, 8), TW), :] = costs_ref[y].astype(F32)

    @pl.loop(0, TW, unroll=8)
    def _(x):
        a = acc[pl.ds(x, TH, stride=PITCH), :].astype(BF16)
        keep(c_h, cq_h, cm_h, x, nt_dot(perm, jnp.concatenate([a] * 4, axis=0)))

    def columns():
        @pl.loop(0, TH, unroll=4)
        def _(y):
            keep(c_v, cq_v, cm_v, y, nt_dot(perm, costs_ref[y]))

    def h_copy(way):
        return pltpu.make_async_remote_copy(
            out_h.at[way], in_h.at[way], send_h.at[way], recv_h.at[way],
            device_id=(row, col + 1 - 2 * way), device_id_type=MESH,
        )

    def v_copy(way):
        return pltpu.make_async_remote_copy(
            out_v.at[way], in_v.at[way], send_v.at[way], recv_v.at[way],
            device_id=(row + 1 - 2 * way, col), device_id_type=MESH,
        )

    def along_row(way):
        at = jnp.where(way == 0, col, cols - 1 - col)

        @pl.when(at == 0)
        def _():
            in_h[way] = jnp.zeros((32, 128), BF16)

        @pl.when(at > 0)
        def _():
            h_copy(way).wait_recv()

        got = in_h[way].astype(F32)
        got = [got[:16], got[16:]]
        turned = [[v] + [pltpu.roll(v, 32 * k, 1) for k in (1, 2, 3)] for v in got]
        v = []
        for g in range(4):
            for i in range(2):
                u = turned[i][-g % 4]
                for h in range(1, 4):
                    u = jnp.where(after[h], turned[i][(h - g) % 4], u)
                v.append(u.astype(BF16))

        def body(t, carry):
            x = jnp.where(way == 0, t, TW - 1 - t)
            v, m = step(*carry, registers(c_h[x]), registers(cq_h[x]), cm_h[x], q1, q1_low, q1_high)
            path_h[way, x] = jnp.concatenate(v, axis=0)
            return v, m

        v, _ = lax.fori_loop(0, TW, body, (v, least(v)), unroll=8)

        @pl.when(at < cols - 1)
        def _():
            packed = []
            for i in range(2):
                u = v[i]
                for g in range(1, 4):
                    u = jnp.where(after[g], v[2 * g + i], u)
                packed.append(u)
            out_h[way] = jnp.concatenate(packed, axis=0)
            h_copy(way).start()

    def along_col(way):
        at = jnp.where(way == 0, row, rows - 1 - row)

        @pl.when(at == 0)
        def _():
            in_v[way] = jnp.zeros((D, 128), BF16)

        @pl.when(at > 0)
        def _():
            v_copy(way).wait_recv()

        v = [a.astype(BF16) for a in registers(in_v[way].astype(F32))]

        def body(t, carry):
            y = jnp.where(way == 0, t, TH - 1 - t)
            v, m = step(*carry, registers(c_v[y]), registers(cq_v[y]), cm_v[y], q1, q1_low, q1_high)
            path_v[way, y] = jnp.concatenate(v, axis=0)
            return v, m

        v, _ = lax.fori_loop(0, TH, body, (v, least(v)), unroll=8)

        @pl.when(at < rows - 1)
        def _():
            out_v[way] = jnp.concatenate(v, axis=0)
            v_copy(way).start()

    missing = sum(jnp.where(there, 0, 1) for there, _, _ in partners)
    pl.semaphore_wait(barrier, 4 - missing)

    near = jnp.minimum(col, cols - 1 - col)
    h_one = jnp.where(col * 2 < cols, 0, 1)
    v_near = jnp.minimum(row, rows - 1 - row)
    v_one = jnp.where(row * 2 < rows, 0, 1)
    before = (near * 3) // 4
    until = before + ((cols - 2 - 2 * near) * 3) // 4

    def add_columns():
        @pl.loop(0, TH, unroll=2)
        def _(y):
            both = jnp.concatenate([path_v[0, y], path_v[1, y]], axis=0)
            both = nn_dot(jnp.concatenate([back, back], axis=1), both)
            acc[pl.ds(pl.multiple_of(y * PITCH, 8), TW), :] = jnp.transpose(both)

    def add_rows(way):
        @pl.loop(0, TW // 4, unroll=8)
        def _(g):
            v = registers(path_h[way, 4 * g])
            for k in range(1, 4):
                v = [jnp.where(after[k], b, a) for a, b in zip(v, registers(path_h[way, 4 * g + k]))]
            v = jnp.transpose(nn_dot(back, jnp.concatenate(v, axis=0)))
            for k in range(4):
                at = pl.ds(4 * g + k, TH, stride=PITCH)
                acc[at, :] = acc[at, :] + v[TH * k : TH * (k + 1)]

    v_late = rows - 1 - v_near >= until

    @pl.loop(0, 9)
    def _(p):
        part, which = p // 3, p % 3
        slot = jnp.where(which == 0, v_near, rows - 1 - v_near)
        v_part = jnp.where(slot < before, 0, jnp.where(slot < until, 1, 2))

        @pl.when(p == jnp.where(near < 2, 3, 0))
        def _():
            columns()

        @pl.when(p == jnp.where(v_late, 8, 5))
        def _():
            add_columns()
            add_rows(h_one)

        @pl.when(jnp.logical_and(which == 2, part < 2))
        def _():
            along_row(jnp.where(part == 0, h_one, 1 - h_one))

        @pl.when(jnp.logical_and(which < 2, v_part == part))
        def _():
            along_col(jnp.where(which == 0, v_one, 1 - v_one))

    add_rows(1 - h_one)

    CH = TH // 4

    def next_tile(q):
        at = pl.ds(q * CH, CH)
        return pltpu.make_async_remote_copy(
            folded.at[at], beyond.at[at], send_b.at[q], recv_b.at[q],
            device_id=(row, col - 1), device_id_type=MESH,
        )

    def write(src, dst, sem, q):
        at = pl.ds(q * CH, CH)
        return pltpu.make_async_copy(src.at[at], dst.at[at], sem.at[q])

    lane32 = lax.broadcasted_iota(jnp.int32, (32, D), 1)

    @pl.loop(0, 4)
    def _(q):
        @pl.loop(q * CH, (q + 1) * CH)
        def _(y):
            v = acc[pl.ds(pl.multiple_of(y * PITCH, 8), TW), :] * (1.0 / 64.0)
            left_ref[y] = v.astype(BF16)
            one = jnp.where(lane32 < 32, pltpu.roll(v[96:], 32, 1), v[32:64])
            two = jnp.where(lane32[:16] < 64, pltpu.roll(v[80:96], 64, 1), v[64:80])
            folded[y] = jnp.concatenate([v[:32], one, two], axis=0).astype(BF16)

        @pl.when(col > 0)
        def _():
            next_tile(q).start()

        write(left_ref, left_out, done_l, q).start()

    @pl.when(col == cols - 1)
    def _():
        beyond[...] = jnp.zeros((TH, FOLD, D), BF16)

    @pl.loop(0, 4)
    def _(q):
        @pl.when(col < cols - 1)
        def _():
            next_tile(q).wait_recv()

        @pl.loop(q * CH, (q + 1) * CH)
        def _(y):
            f = beyond[y].astype(F32)
            v = jnp.concatenate(
                [left_ref[y].astype(F32), f, pltpu.roll(f[64:80], 64, 1), pltpu.roll(f[32:64], 96, 1)], axis=0
            )
            for bit, size in ((64, 192), (32, 160), (16, 144), (8, 136)):
                d = lax.broadcasted_iota(jnp.int32, (size, D), 1)
                v = jnp.where((d & bit) != 0, v[bit : bit + size], v[:size])
            d = lax.broadcasted_iota(jnp.int32, (136, D), 1)
            for bit in (4, 2, 1):
                v = jnp.where((d & bit) != 0, pltpu.roll(v, 136 - bit, 0), v)
            right_ref[y] = v[:TW].astype(BF16)

        write(right_ref, right_out, done_r, q).start()

    for q in range(4):
        write(left_ref, left_out, done_l, q).wait()
        write(right_ref, right_out, done_r, q).wait()

    for way in (0, 1):
        at_h = col if way == 0 else cols - 1 - col
        at_v = row if way == 0 else rows - 1 - row

        @pl.when(at_h < cols - 1)
        def _(way=way):
            h_copy(way).wait_send()

        @pl.when(at_v < rows - 1)
        def _(way=way):
            v_copy(way).wait_send()

    @pl.when(col > 0)
    def _():
        for q in range(4):
            next_tile(q).wait_send()


def shards(costs, p_small, p_large):
    tile = jax.ShapeDtypeStruct(costs.shape, BF16)
    return pl.pallas_call(
        kernel,
        out_shape=(tile, tile),
        in_specs=[
            pl.BlockSpec(memory_space=pltpu.SMEM),
            pl.BlockSpec(memory_space=pltpu.SMEM),
            pl.BlockSpec(memory_space=pltpu.VMEM),
        ],
        out_specs=(pl.BlockSpec(memory_space=pl.ANY), pl.BlockSpec(memory_space=pl.ANY)),
        scratch_shapes=[
            pltpu.VMEM((TH, TW, D), BF16),
            pltpu.VMEM((TH, TW, D), BF16),
            pltpu.VMEM((TH, FOLD, D), BF16),
            pltpu.VMEM((TW, D, 128), BF16),
            pltpu.VMEM((TW, D, 128), BF16),
            pltpu.VMEM((TW, 8, 128), F32),
            pltpu.VMEM((TH, D, 128), BF16),
            pltpu.VMEM((TH, D, 128), BF16),
            pltpu.VMEM((TH, 8, 128), F32),
            pltpu.VMEM((2, TW, D, 128), BF16),
            pltpu.VMEM((2, TH, D, 128), BF16),
            pltpu.VMEM((TH * PITCH, D), F32),
            pltpu.VMEM((TH, FOLD, D), BF16),
            pltpu.VMEM((2, 32, 128), BF16),
            pltpu.VMEM((2, 32, 128), BF16),
            pltpu.VMEM((2, D, 128), BF16),
            pltpu.VMEM((2, D, 128), BF16),
            pltpu.SemaphoreType.DMA((2,)),
            pltpu.SemaphoreType.DMA((2,)),
            pltpu.SemaphoreType.DMA((2,)),
            pltpu.SemaphoreType.DMA((2,)),
            pltpu.SemaphoreType.DMA((4,)),
            pltpu.SemaphoreType.DMA((4,)),
            pltpu.SemaphoreType.DMA((4,)),
            pltpu.SemaphoreType.DMA((4,)),
        ],
        compiler_params=pltpu.CompilerParams(collective_id=0, has_side_effects=True),
        name="sgm",
    )(p_small, p_large, costs)


def solution(mesh):
    placed = (P("row", "col", None), P(), P())
    return jax.shard_map(
        shards,
        mesh=mesh,
        in_specs=placed,
        out_specs=(P("row", "col", None), P("row", "col", None)),
        check_vma=False,
    )
```

```python
import jax
import jax.numpy as jnp
from jax import lax
from jax.experimental import pallas as pl
from jax.experimental.pallas import tpu as pltpu
from jax.sharding import PartitionSpec as P

MESH = pl.DeviceIdType.MESH
F32 = jnp.float32
BF16 = jnp.bfloat16
FAR = 1.0e9

TH, TW, D = 32, 128, 128
NJ = 8
PITCH = 136


def nt_dot(a, b):
    return lax.dot_general(a, b, (((1,), (1,)), ((), ())), preferred_element_type=F32)


def nn_dot(a, b):
    return lax.dot_general(a, b, (((1,), (0,)), ((), ())), preferred_element_type=F32)


def registers(slab):
    return [slab[16 * j : 16 * j + 16] for j in range(NJ)]


def least(parts):
    parts = list(parts)
    while len(parts) > 1:
        parts = [jnp.minimum(parts[i], parts[i + 1]) for i in range(0, len(parts), 2)]
    m = parts[0].astype(F32)
    m = jnp.minimum(m[:8], m[8:])
    for s in (4, 2, 1):
        m = jnp.minimum(m, pltpu.roll(m, s, 0))
    return m


def step(v, m, c, cq, cm, q1, q1_low, q1_high):
    low = pltpu.roll(v[NJ - 1], 1, 0) + q1_low
    high = pltpu.roll(v[0], 15, 0) + q1_high
    w = []
    for j in range(NJ):
        if j == 0:
            sides = jnp.minimum(low, v[1] + q1)
        elif j == NJ - 1:
            sides = jnp.minimum(high, v[NJ - 2] + q1)
        else:
            sides = jnp.minimum(v[j - 1], v[j + 1]) + q1
        w.append(jnp.minimum(v[j], sides) + c[j])
    a = least([w[1], w[2], w[3], w[4], w[5], w[6], w[0], w[7]])
    whole = jnp.concatenate([m, m], axis=0).astype(BF16)
    return [jnp.minimum(w[j] - whole, cq[j]) for j in range(NJ)], jnp.minimum(a - m, cm)


def kernel(
    small_ref, large_ref, costs_ref, left_out, right_out, left_ref, right_ref,
    send_0, send_1, send_2, send_3, beyond_0, beyond_1, beyond_2, beyond_3, state, state_low,
    c_h, cq_h, cm_h, c_v, cq_v, cm_v, path_h, path_v, acc,
    out_h, in_h, out_v, in_v, send_h, recv_h, send_v, recv_v, send_b, recv_b, done_l, done_r,
):
    row, col = lax.axis_index("row"), lax.axis_index("col")
    rows, cols = lax.axis_size("row"), lax.axis_size("col")

    barrier = pltpu.get_barrier_semaphore()
    partners = [
        (col > 0, row, col - 1),
        (col < cols - 1, row, col + 1),
        (row > 0, row - 1, col),
        (row < rows - 1, row + 1, col),
    ]
    for there, r, c in partners:

        @pl.when(there)
        def _(r=r, c=c):
            pl.semaphore_signal(barrier, inc=1, device_id=(r, c), device_id_type=MESH)


    q1f = jnp.full((16, 128), small_ref[0].astype(F32))
    q2f = jnp.full((16, 128), large_ref[0].astype(F32))
    sub = lax.broadcasted_iota(jnp.int32, (16, 128), 0)
    q1, q2 = q1f.astype(BF16), q2f.astype(BF16)
    q1_low = jnp.where(sub == 0, FAR, q1f).astype(BF16)
    q1_high = jnp.where(sub == 15, FAR, q1f).astype(BF16)
    lane = lax.broadcasted_iota(jnp.int32, (16, 128), 1)
    after = [lane >= 32 * h for h in range(4)]
    r0 = lax.broadcasted_iota(jnp.int32, (D, D), 0)
    r1 = lax.broadcasted_iota(jnp.int32, (D, D), 1)
    perm = (r1 == (r0 % 16) * 8 + r0 // 16).astype(F32).astype(BF16)
    back = (r0 == (r1 % 16) * 8 + r1 // 16).astype(F32).astype(BF16)

    def keep(c_ref, cq_ref, cm_ref, n, slab):
        slab = slab.astype(BF16)
        cq = [c + q2 for c in registers(slab)]
        c_ref[n] = slab
        cq_ref[n] = jnp.concatenate(cq, axis=0)
        cm_ref[n] = least(cq)

    @pl.loop(0, TH)
    def _(y):
        acc[pl.ds(pl.multiple_of(y * PITCH, 8), TW), :] = costs_ref[y].astype(F32)

    @pl.loop(0, TW, unroll=16)
    def _(x):
        a = acc[pl.ds(x, TH, stride=PITCH), :].astype(BF16)
        keep(c_h, cq_h, cm_h, x, nt_dot(perm, jnp.concatenate([a] * 4, axis=0)))

    def columns():
        @pl.loop(0, TH, unroll=4)
        def _(y):
            keep(c_v, cq_v, cm_v, y, nt_dot(perm, costs_ref[y]))

    def h_copy(way):
        return pltpu.make_async_remote_copy(
            out_h.at[way], in_h.at[way], send_h.at[way], recv_h.at[way],
            device_id=(row, col + 1 - 2 * way), device_id_type=MESH,
        )

    def v_copy(way):
        return pltpu.make_async_remote_copy(
            out_v.at[way], in_v.at[way], send_v.at[way], recv_v.at[way],
            device_id=(row + 1 - 2 * way, col), device_id_type=MESH,
        )

    def arrived(way, at):
        @pl.when(at == 0)
        def _():
            in_h[way] = jnp.zeros((32, 128), BF16)

        @pl.when(at > 0)
        def _():
            h_copy(way).wait_recv()

        got = in_h[way].astype(F32)
        got = [got[:16], got[16:]]
        turned = [[v] + [pltpu.roll(v, 32 * k, 1) for k in (1, 2, 3)] for v in got]
        v = []
        for g in range(4):
            for i in range(2):
                u = turned[i][-g % 4]
                for h in range(1, 4):
                    u = jnp.where(after[h], turned[i][(h - g) % 4], u)
                v.append(u)
        return v

    def run_row(way, start, count, v, m):
        def body(t, carry):
            x = jnp.where(way == 0, start + t, TW - 1 - start - t)
            v, m = step(*carry, registers(c_h[x]), registers(cq_h[x]), cm_h[x], q1, q1_low, q1_high)
            path_h[way, x] = jnp.concatenate(v, axis=0)
            return v, m

        return lax.fori_loop(0, count, body, (v, m), unroll=8)

    def along_row(way):
        at = jnp.where(way == 0, col, cols - 1 - col)
        v = [a.astype(BF16) for a in arrived(way, at)]
        v, _ = run_row(way, 0, TW, v, least(v))

        @pl.when(at < cols - 1)
        def _():
            packed = []
            for i in range(2):
                u = v[i]
                for g in range(1, 4):
                    u = jnp.where(after[g], v[2 * g + i], u)
                packed.append(u)
            out_h[way] = jnp.concatenate(packed, axis=0)
            h_copy(way).start()

    def along_col(way):
        at = jnp.where(way == 0, row, rows - 1 - row)

        @pl.when(at == 0)
        def _():
            in_v[way] = jnp.zeros((D, 128), BF16)

        @pl.when(at > 0)
        def _():
            v_copy(way).wait_recv()

        v = [a.astype(BF16) for a in registers(in_v[way].astype(F32))]

        def body(t, carry):
            y = jnp.where(way == 0, t, TH - 1 - t)
            v, m = step(*carry, registers(c_v[y]), registers(cq_v[y]), cm_v[y], q1, q1_low, q1_high)
            path_v[way, y] = jnp.concatenate(v, axis=0)
            return v, m

        v, _ = lax.fori_loop(0, TH, body, (v, least(v)), unroll=8)

        @pl.when(at < rows - 1)
        def _():
            out_v[way] = jnp.concatenate(v, axis=0)
            v_copy(way).start()

    missing = sum(jnp.where(there, 0, 1) for there, _, _ in partners)
    pl.semaphore_wait(barrier, 4 - missing)

    near = jnp.minimum(col, cols - 1 - col)
    h_one = jnp.where(col * 2 < cols, 0, 1)
    v_near = jnp.minimum(row, rows - 1 - row)
    v_one = jnp.where(row * 2 < rows, 0, 1)
    before = jnp.minimum((near * 3) // 4, 4)
    until = before + ((cols - 2 - 2 * near) * 3) // 4

    def add_columns():
        @pl.loop(0, TH, unroll=2)
        def _(y):
            both = jnp.concatenate([path_v[0, y], path_v[1, y]], axis=0)
            both = nn_dot(jnp.concatenate([back, back], axis=1), both)
            acc[pl.ds(pl.multiple_of(y * PITCH, 8), TW), :] = jnp.transpose(both)

    def add_rows(way, start, count):
        @pl.loop(0, count, unroll=8)
        def _(n):
            g = start + n
            v = registers(path_h[way, 4 * g])
            for k in range(1, 4):
                v = [jnp.where(after[k], b, a) for a, b in zip(v, registers(path_h[way, 4 * g + k]))]
            v = jnp.transpose(nn_dot(back, jnp.concatenate(v, axis=0)))
            for k in range(4):
                at = pl.ds(4 * g + k, TH, stride=PITCH)
                acc[at, :] = acc[at, :] + v[TH * k : TH * (k + 1)]

    v_late = rows - 1 - v_near >= until

    @pl.loop(0, 9)
    def _(p):
        part, which = p // 3, p % 3
        slot = jnp.where(which == 0, v_near, rows - 1 - v_near)
        v_part = jnp.where(slot < before, 0, jnp.where(slot < until, 1, 2))

        @pl.when(p == jnp.where(near < 2, 3, 0))
        def _():
            columns()

        @pl.when(p == jnp.where(v_late, 8, 5))
        def _():
            add_columns()
            add_rows(h_one, 0, TW // 4)

        @pl.when(jnp.logical_and(which == 2, jnp.logical_or(part == 0, jnp.logical_and(part == 1, near > 0))))
        def _():
            along_row(jnp.where(part == 0, h_one, 1 - h_one))

        @pl.when(jnp.logical_and(which < 2, v_part == part))
        def _():
            along_col(jnp.where(which == 0, v_one, 1 - v_one))

    CW = TW // 4
    last = 1 - h_one
    ends = near == 0
    lane32 = lax.broadcasted_iota(jnp.int32, (CW, D), 1)
    blocks = ((send_0, beyond_0), (send_1, beyond_1), (send_2, beyond_2), (send_3, beyond_3))

    def next_tile(q):
        return pltpu.make_async_remote_copy(
            blocks[q][0], blocks[q][1], send_b.at[q], recv_b.at[q],
            device_id=(row, col - 1), device_id_type=MESH,
        )

    def write(src, dst, sem, q):
        at = pl.ds(q * CW, CW)
        return pltpu.make_async_copy(src.at[:, at], dst.at[:, at], sem.at[q])

    def fold(q, v):
        if q == 2:
            return jnp.where(lane32[:16] < 64, pltpu.roll(v[16:], 64, 1), v[:16])
        if q == 3:
            u = v[:8]
            for k in (1, 2, 3):
                u = jnp.where(lane32[:8] < 128 - 32 * k, pltpu.roll(v[8 * k : 8 * k + 8], 128 - 32 * k, 1), u)
            return u
        return v

    def unfold(q, f):
        if q == 2:
            return [f, pltpu.roll(f, 64, 1)]
        if q == 3:
            return [f] + [pltpu.roll(f, 32 * k, 1) for k in (1, 2, 3)]
        return [f]

    @pl.when(ends)
    def _():
        v = arrived(last, cols - 1)
        state[...] = jnp.concatenate(v, axis=0)
        state_low[...] = least([a.astype(BF16) for a in v])

    @pl.loop(0, 4)
    def _(n):
        now = jnp.where(jnp.logical_and(ends, last == 1), 3 - n, n)

        @pl.when(ends)
        def _():
            v = [a.astype(BF16) for a in registers(state[...])]
            v, m = run_row(last, n * CW, CW, v, state_low[...])
            state[...] = jnp.concatenate([a.astype(F32) for a in v], axis=0)
            state_low[...] = m

        add_rows(last, now * (CW // 4), CW // 4)

        for q in range(4):

            @pl.when(now == q)
            def _(q=q):
                @pl.loop(0, TH, unroll=4)
                def _(y):
                    v = acc[pl.ds(pl.multiple_of(y * PITCH + q * CW, 8), CW), :] * (1.0 / 64.0)
                    left_ref[y, q * CW : (q + 1) * CW] = v.astype(BF16)
                    blocks[q][0][y] = fold(q, v).astype(BF16)

                @pl.when(col > 0)
                def _():
                    next_tile(q).start()

                write(left_ref, left_out, done_l, q).start()

    @pl.when(col == cols - 1)
    def _():
        for _, b in blocks:
            b[...] = jnp.zeros(b.shape, BF16)

    for p in range(4):

        @pl.when(col < cols - 1)
        def _(p=p):
            next_tile(p).wait_recv()

        @pl.loop(0, TH, unroll=2)
        def _(y, p=p):
            v = [left_ref[y, p * CW :].astype(F32)]
            for q in range(p + 1):
                v += unfold(q, blocks[q][1][y].astype(F32))
            v = jnp.concatenate(v, axis=0)
            for bit, size in ((64, 96), (32, 64), (16, 48), (8, 40)):
                d = lax.broadcasted_iota(jnp.int32, (size, D), 1)
                v = jnp.where((d & bit) != 0, v[bit : bit + size], v[:size])
            d = lax.broadcasted_iota(jnp.int32, (40, D), 1)
            for bit in (4, 2, 1):
                v = jnp.where((d & bit) != 0, pltpu.roll(v, 40 - bit, 0), v)
            right_ref[y, p * CW : (p + 1) * CW] = v[:CW].astype(BF16)

        write(right_ref, right_out, done_r, p).start()

    for q in range(4):
        write(left_ref, left_out, done_l, q).wait()
        write(right_ref, right_out, done_r, q).wait()

    for way in (0, 1):
        at_h = col if way == 0 else cols - 1 - col
        at_v = row if way == 0 else rows - 1 - row

        @pl.when(at_h < cols - 1)
        def _(way=way):
            h_copy(way).wait_send()

        @pl.when(at_v < rows - 1)
        def _(way=way):
            v_copy(way).wait_send()

    @pl.when(col > 0)
    def _():
        for q in range(4):
            next_tile(q).wait_send()


def shards(costs, p_small, p_large):
    tile = jax.ShapeDtypeStruct(costs.shape, BF16)
    return pl.pallas_call(
        kernel,
        out_shape=(tile, tile),
        in_specs=[
            pl.BlockSpec(memory_space=pltpu.SMEM),
            pl.BlockSpec(memory_space=pltpu.SMEM),
            pl.BlockSpec(memory_space=pltpu.VMEM),
        ],
        out_specs=(pl.BlockSpec(memory_space=pl.ANY), pl.BlockSpec(memory_space=pl.ANY)),
        scratch_shapes=[
            pltpu.VMEM((TH, TW, D), BF16),
            pltpu.VMEM((TH, TW, D), BF16),
            *[pltpu.VMEM((TH, n, D), BF16) for n in (32, 32, 16, 8)],
            *[pltpu.VMEM((TH, n, D), BF16) for n in (32, 32, 16, 8)],
            pltpu.VMEM((D, 128), F32),
            pltpu.VMEM((8, 128), F32),
            pltpu.VMEM((TW, D, 128), BF16),
            pltpu.VMEM((TW, D, 128), BF16),
            pltpu.VMEM((TW, 8, 128), F32),
            pltpu.VMEM((TH, D, 128), BF16),
            pltpu.VMEM((TH, D, 128), BF16),
            pltpu.VMEM((TH, 8, 128), F32),
            pltpu.VMEM((2, TW, D, 128), BF16),
            pltpu.VMEM((2, TH, D, 128), BF16),
            pltpu.VMEM((TH * PITCH, D), F32),
            pltpu.VMEM((2, 32, 128), BF16),
            pltpu.VMEM((2, 32, 128), BF16),
            pltpu.VMEM((2, D, 128), BF16),
            pltpu.VMEM((2, D, 128), BF16),
            pltpu.SemaphoreType.DMA((2,)),
            pltpu.SemaphoreType.DMA((2,)),
            pltpu.SemaphoreType.DMA((2,)),
            pltpu.SemaphoreType.DMA((2,)),
            pltpu.SemaphoreType.DMA((4,)),
            pltpu.SemaphoreType.DMA((4,)),
            pltpu.SemaphoreType.DMA((4,)),
            pltpu.SemaphoreType.DMA((4,)),
        ],
        compiler_params=pltpu.CompilerParams(collective_id=0, has_side_effects=True),
        name="sgm",
    )(p_small, p_large, costs)


def solution(mesh):
    placed = (P("row", "col", None), P(), P())
    return jax.shard_map(
        shards,
        mesh=mesh,
        in_specs=placed,
        out_specs=(P("row", "col", None), P("row", "col", None)),
        check_vma=False,
    )
```

```python
import jax
import jax.numpy as jnp
from jax import lax
from jax.experimental import pallas as pl
from jax.experimental.pallas import tpu as pltpu
from jax.sharding import PartitionSpec as P

MESH = pl.DeviceIdType.MESH
F32 = jnp.float32
BF16 = jnp.bfloat16
FAR = 1.0e9

TH, TW, D = 32, 128, 128
NJ = 8
PITCH = 136


def nt_dot(a, b):
    return lax.dot_general(a, b, (((1,), (1,)), ((), ())), preferred_element_type=F32)


def nn_dot(a, b):
    return lax.dot_general(a, b, (((1,), (0,)), ((), ())), preferred_element_type=F32)


def registers(slab):
    return [slab[16 * j : 16 * j + 16] for j in range(NJ)]


def least(parts):
    parts = list(parts)
    while len(parts) > 1:
        parts = [jnp.minimum(parts[i], parts[i + 1]) for i in range(0, len(parts), 2)]
    m = parts[0].astype(F32)
    m = jnp.minimum(m[:8], m[8:])
    for s in (4, 2, 1):
        m = jnp.minimum(m, pltpu.roll(m, s, 0))
    return m


def step(v, m, c, cq, cm, q1, q1_low, q1_high):
    low = pltpu.roll(v[NJ - 1], 1, 0) + q1_low
    high = pltpu.roll(v[0], 15, 0) + q1_high
    w = []
    for j in range(NJ):
        if j == 0:
            sides = jnp.minimum(low, v[1] + q1)
        elif j == NJ - 1:
            sides = jnp.minimum(high, v[NJ - 2] + q1)
        else:
            sides = jnp.minimum(v[j - 1], v[j + 1]) + q1
        w.append(jnp.minimum(v[j], sides) + c[j])
    a = least([w[1], w[2], w[3], w[4], w[5], w[6], w[0], w[7]])
    whole = jnp.concatenate([m, m], axis=0).astype(BF16)
    return [jnp.minimum(w[j] - whole, cq[j]) for j in range(NJ)], jnp.minimum(a - m, cm)


def kernel(
    small_ref, large_ref, costs_ref, left_ref, right_ref,
    send_0, send_1, send_2, send_3, beyond_0, beyond_1, beyond_2, beyond_3, state, state_low,
    c_h, cq_h, cm_h, c_v, cq_v, cm_v, path_h, path_v, acc,
    out_h, in_h, out_v, in_v, send_h, recv_h, send_v, recv_v, send_b, recv_b,
):
    row, col = lax.axis_index("row"), lax.axis_index("col")
    rows, cols = lax.axis_size("row"), lax.axis_size("col")

    barrier = pltpu.get_barrier_semaphore()
    partners = [
        (col > 0, row, col - 1),
        (col < cols - 1, row, col + 1),
        (row > 0, row - 1, col),
        (row < rows - 1, row + 1, col),
    ]
    for there, r, c in partners:

        @pl.when(there)
        def _(r=r, c=c):
            pl.semaphore_signal(barrier, inc=1, device_id=(r, c), device_id_type=MESH)


    q1f = jnp.full((16, 128), small_ref[0].astype(F32))
    q2f = jnp.full((16, 128), large_ref[0].astype(F32))
    sub = lax.broadcasted_iota(jnp.int32, (16, 128), 0)
    q1, q2 = q1f.astype(BF16), q2f.astype(BF16)
    q1_low = jnp.where(sub == 0, FAR, q1f).astype(BF16)
    q1_high = jnp.where(sub == 15, FAR, q1f).astype(BF16)
    lane = lax.broadcasted_iota(jnp.int32, (16, 128), 1)
    after = [lane >= 32 * h for h in range(4)]
    r0 = lax.broadcasted_iota(jnp.int32, (D, D), 0)
    r1 = lax.broadcasted_iota(jnp.int32, (D, D), 1)
    perm = (r1 == (r0 % 16) * 8 + r0 // 16).astype(F32).astype(BF16)
    back = (r0 == (r1 % 16) * 8 + r1 // 16).astype(F32).astype(BF16)

    def keep(c_ref, cq_ref, cm_ref, n, slab):
        slab = slab.astype(BF16)
        cq = [c + q2 for c in registers(slab)]
        c_ref[n] = slab
        cq_ref[n] = jnp.concatenate(cq, axis=0)
        cm_ref[n] = least(cq)

    @pl.loop(0, TH)
    def _(y):
        acc[pl.ds(pl.multiple_of(y * PITCH, 8), TW), :] = costs_ref[y].astype(F32)

    @pl.loop(0, TW, unroll=16)
    def _(x):
        a = acc[pl.ds(x, TH, stride=PITCH), :].astype(BF16)
        keep(c_h, cq_h, cm_h, x, nt_dot(perm, jnp.concatenate([a] * 4, axis=0)))

    def columns():
        @pl.loop(0, TH, unroll=4)
        def _(y):
            keep(c_v, cq_v, cm_v, y, nt_dot(perm, costs_ref[y]))

    def h_copy(way):
        return pltpu.make_async_remote_copy(
            out_h.at[way], in_h.at[way], send_h.at[way], recv_h.at[way],
            device_id=(row, col + 1 - 2 * way), device_id_type=MESH,
        )

    def v_copy(way):
        return pltpu.make_async_remote_copy(
            out_v.at[way], in_v.at[way], send_v.at[way], recv_v.at[way],
            device_id=(row + 1 - 2 * way, col), device_id_type=MESH,
        )

    def arrived(way, at):
        @pl.when(at == 0)
        def _():
            in_h[way] = jnp.zeros((32, 128), BF16)

        @pl.when(at > 0)
        def _():
            h_copy(way).wait_recv()

        got = in_h[way].astype(F32)
        got = [got[:16], got[16:]]
        turned = [[v] + [pltpu.roll(v, 32 * k, 1) for k in (1, 2, 3)] for v in got]
        v = []
        for g in range(4):
            for i in range(2):
                u = turned[i][-g % 4]
                for h in range(1, 4):
                    u = jnp.where(after[h], turned[i][(h - g) % 4], u)
                v.append(u)
        return v

    def run_row(way, start, count, v, m):
        def body(t, carry):
            x = jnp.where(way == 0, start + t, TW - 1 - start - t)
            v, m = step(*carry, registers(c_h[x]), registers(cq_h[x]), cm_h[x], q1, q1_low, q1_high)
            path_h[way, x] = jnp.concatenate(v, axis=0)
            return v, m

        return lax.fori_loop(0, count, body, (v, m), unroll=16)

    def along_row(way):
        at = jnp.where(way == 0, col, cols - 1 - col)
        v = [a.astype(BF16) for a in arrived(way, at)]
        v, _ = run_row(way, 0, TW, v, least(v))

        @pl.when(at < cols - 1)
        def _():
            packed = []
            for i in range(2):
                u = v[i]
                for g in range(1, 4):
                    u = jnp.where(after[g], v[2 * g + i], u)
                packed.append(u)
            out_h[way] = jnp.concatenate(packed, axis=0)
            h_copy(way).start()

    def along_col(way):
        at = jnp.where(way == 0, row, rows - 1 - row)

        @pl.when(at == 0)
        def _():
            in_v[way] = jnp.zeros((D, 128), BF16)

        @pl.when(at > 0)
        def _():
            v_copy(way).wait_recv()

        v = [a.astype(BF16) for a in registers(in_v[way].astype(F32))]

        def body(t, carry):
            y = jnp.where(way == 0, t, TH - 1 - t)
            v, m = step(*carry, registers(c_v[y]), registers(cq_v[y]), cm_v[y], q1, q1_low, q1_high)
            path_v[way, y] = jnp.concatenate(v, axis=0)
            return v, m

        v, _ = lax.fori_loop(0, TH, body, (v, least(v)), unroll=8)

        @pl.when(at < rows - 1)
        def _():
            out_v[way] = jnp.concatenate(v, axis=0)
            v_copy(way).start()

    missing = sum(jnp.where(there, 0, 1) for there, _, _ in partners)
    pl.semaphore_wait(barrier, 4 - missing)

    near = jnp.minimum(col, cols - 1 - col)
    h_one = jnp.where(col * 2 < cols, 0, 1)
    v_near = jnp.minimum(row, rows - 1 - row)
    v_one = jnp.where(row * 2 < rows, 0, 1)
    before = jnp.minimum((near * 3) // 4, 4)
    until = before + ((cols - 2 - 2 * near) * 3) // 4

    def add_columns():
        @pl.loop(0, TH, unroll=2)
        def _(y):
            both = jnp.concatenate([path_v[0, y], path_v[1, y]], axis=0)
            both = nn_dot(jnp.concatenate([back, back], axis=1), both)
            acc[pl.ds(pl.multiple_of(y * PITCH, 8), TW), :] = jnp.transpose(both)

    def add_rows(way, start, count):
        @pl.loop(0, count, unroll=8)
        def _(n):
            g = start + n
            v = registers(path_h[way, 4 * g])
            for k in range(1, 4):
                v = [jnp.where(after[k], b, a) for a, b in zip(v, registers(path_h[way, 4 * g + k]))]
            v = jnp.transpose(nn_dot(back, jnp.concatenate(v, axis=0)))
            for k in range(4):
                at = pl.ds(4 * g + k, TH, stride=PITCH)
                acc[at, :] = acc[at, :] + v[TH * k : TH * (k + 1)]

    v_late = rows - 1 - v_near >= until

    @pl.loop(0, 9)
    def _(p):
        part, which = p // 3, p % 3
        slot = jnp.where(which == 0, v_near, rows - 1 - v_near)
        v_part = jnp.where(slot < before, 0, jnp.where(slot < until, 1, 2))

        @pl.when(p == jnp.where(near < 2, 3, 0))
        def _():
            columns()

        @pl.when(p == jnp.where(v_late, 8, 5))
        def _():
            add_columns()
            add_rows(h_one, 0, TW // 4)

        @pl.when(jnp.logical_and(which == 2, jnp.logical_or(part == 0, jnp.logical_and(part == 1, near > 0))))
        def _():
            along_row(jnp.where(part == 0, h_one, 1 - h_one))

        @pl.when(jnp.logical_and(which < 2, v_part == part))
        def _():
            along_col(jnp.where(which == 0, v_one, 1 - v_one))

    CW = TW // 4
    last = 1 - h_one
    ends = near == 0
    lane32 = lax.broadcasted_iota(jnp.int32, (CW, D), 1)
    blocks = ((send_0, beyond_0), (send_1, beyond_1), (send_2, beyond_2), (send_3, beyond_3))

    def next_tile(q):
        return pltpu.make_async_remote_copy(
            blocks[q][0], blocks[q][1], send_b.at[q], recv_b.at[q],
            device_id=(row, col - 1), device_id_type=MESH,
        )

    def fold(q, v):
        if q == 2:
            return jnp.where(lane32[:16] < 64, pltpu.roll(v[16:], 64, 1), v[:16])
        if q == 3:
            u = v[:8]
            for k in (1, 2, 3):
                u = jnp.where(lane32[:8] < 128 - 32 * k, pltpu.roll(v[8 * k : 8 * k + 8], 128 - 32 * k, 1), u)
            return u
        return v

    def unfold(q, f):
        if q == 2:
            return [f, pltpu.roll(f, 64, 1)]
        if q == 3:
            return [f] + [pltpu.roll(f, 32 * k, 1) for k in (1, 2, 3)]
        return [f]

    @pl.when(ends)
    def _():
        v = arrived(last, cols - 1)
        state[...] = jnp.concatenate(v, axis=0)
        state_low[...] = least([a.astype(BF16) for a in v])

    @pl.loop(0, 4)
    def _(n):
        now = jnp.where(jnp.logical_and(ends, last == 1), 3 - n, n)

        @pl.when(ends)
        def _():
            v = [a.astype(BF16) for a in registers(state[...])]
            v, m = run_row(last, n * CW, CW, v, state_low[...])
            state[...] = jnp.concatenate([a.astype(F32) for a in v], axis=0)
            state_low[...] = m

        add_rows(last, now * (CW // 4), CW // 4)

        for q in range(4):

            @pl.when(now == q)
            def _(q=q):
                @pl.loop(0, TH, unroll=4)
                def _(y):
                    v = acc[pl.ds(pl.multiple_of(y * PITCH + q * CW, 8), CW), :] * (1.0 / 64.0)
                    left_ref[y, q * CW : (q + 1) * CW] = v.astype(BF16)
                    blocks[q][0][y] = fold(q, v).astype(BF16)

                @pl.when(col > 0)
                def _():
                    next_tile(q).start()


    @pl.when(col == cols - 1)
    def _():
        for _, b in blocks:
            b[...] = jnp.zeros(b.shape, BF16)

    for p in range(4):

        @pl.when(col < cols - 1)
        def _(p=p):
            next_tile(p).wait_recv()

        @pl.loop(0, TH, unroll=2)
        def _(y, p=p):
            v = [left_ref[y, p * CW :].astype(F32)]
            for q in range(p + 1):
                v += unfold(q, blocks[q][1][y].astype(F32))
            v = jnp.concatenate(v, axis=0)
            for bit, size in ((64, 96), (32, 64), (16, 48), (8, 40)):
                d = lax.broadcasted_iota(jnp.int32, (size, D), 1)
                v = jnp.where((d & bit) != 0, v[bit : bit + size], v[:size])
            d = lax.broadcasted_iota(jnp.int32, (40, D), 1)
            for bit in (4, 2, 1):
                v = jnp.where((d & bit) != 0, pltpu.roll(v, 40 - bit, 0), v)
            right_ref[y, p * CW : (p + 1) * CW] = v[:CW].astype(BF16)

    for way in (0, 1):
        at_h = col if way == 0 else cols - 1 - col
        at_v = row if way == 0 else rows - 1 - row

        @pl.when(at_h < cols - 1)
        def _(way=way):
            h_copy(way).wait_send()

        @pl.when(at_v < rows - 1)
        def _(way=way):
            v_copy(way).wait_send()

    @pl.when(col > 0)
    def _():
        for q in range(4):
            next_tile(q).wait_send()


def put(left_ref, right_ref, left_out, right_out, sem):
    one = pltpu.make_async_copy(left_ref, left_out, sem.at[0])
    two = pltpu.make_async_copy(right_ref, right_out, sem.at[1])
    one.start()
    two.start()
    one.wait()
    two.wait()


def shards(costs, p_small, p_large):
    tile = jax.ShapeDtypeStruct(costs.shape, BF16)
    left, right = pl.pallas_call(
        kernel,
        out_shape=(pltpu.VMEM(costs.shape, BF16), pltpu.VMEM(costs.shape, BF16)),
        in_specs=[
            pl.BlockSpec(memory_space=pltpu.SMEM),
            pl.BlockSpec(memory_space=pltpu.SMEM),
            pl.BlockSpec(memory_space=pltpu.VMEM),
        ],
        out_specs=(pl.BlockSpec(memory_space=pltpu.VMEM), pl.BlockSpec(memory_space=pltpu.VMEM)),
        scratch_shapes=[
            *[pltpu.VMEM((TH, n, D), BF16) for n in (32, 32, 16, 8)],
            *[pltpu.VMEM((TH, n, D), BF16) for n in (32, 32, 16, 8)],
            pltpu.VMEM((D, 128), F32),
            pltpu.VMEM((8, 128), F32),
            pltpu.VMEM((TW, D, 128), BF16),
            pltpu.VMEM((TW, D, 128), BF16),
            pltpu.VMEM((TW, 8, 128), F32),
            pltpu.VMEM((TH, D, 128), BF16),
            pltpu.VMEM((TH, D, 128), BF16),
            pltpu.VMEM((TH, 8, 128), F32),
            pltpu.VMEM((2, TW, D, 128), BF16),
            pltpu.VMEM((2, TH, D, 128), BF16),
            pltpu.VMEM((TH * PITCH, D), F32),
            pltpu.VMEM((2, 32, 128), BF16),
            pltpu.VMEM((2, 32, 128), BF16),
            pltpu.VMEM((2, D, 128), BF16),
            pltpu.VMEM((2, D, 128), BF16),
            pltpu.SemaphoreType.DMA((2,)),
            pltpu.SemaphoreType.DMA((2,)),
            pltpu.SemaphoreType.DMA((2,)),
            pltpu.SemaphoreType.DMA((2,)),
            pltpu.SemaphoreType.DMA((4,)),
            pltpu.SemaphoreType.DMA((4,)),
        ],
        compiler_params=pltpu.CompilerParams(collective_id=0, has_side_effects=True, vmem_limit_bytes=48 << 20),
        name="sgm",
    )(p_small, p_large, costs)
    return pl.pallas_call(
        put,
        out_shape=(tile, tile),
        in_specs=[pl.BlockSpec(memory_space=pltpu.VMEM)] * 2,
        out_specs=(pl.BlockSpec(memory_space=pl.ANY), pl.BlockSpec(memory_space=pl.ANY)),
        scratch_shapes=[pltpu.SemaphoreType.DMA((2,))],
        compiler_params=pltpu.CompilerParams(vmem_limit_bytes=8 << 20),
        name="put",
    )(left, right)


def solution(mesh):
    placed = (P("row", "col", None), P(), P())
    return jax.shard_map(
        shards,
        mesh=mesh,
        in_specs=placed,
        out_specs=(P("row", "col", None), P("row", "col", None)),
        check_vma=False,
    )
```

```python
import jax
import jax.numpy as jnp
from jax import lax
from jax.experimental import pallas as pl
from jax.experimental.pallas import tpu as pltpu
from jax.sharding import PartitionSpec as P

MESH = pl.DeviceIdType.MESH
F32 = jnp.float32
BF16 = jnp.bfloat16
FAR = 1.0e9

TH, TW, D = 32, 128, 128
NJ = 8
PITCH = 136


def nt_dot(a, b):
    return lax.dot_general(a, b, (((1,), (1,)), ((), ())), preferred_element_type=F32)


def nn_dot(a, b):
    return lax.dot_general(a, b, (((1,), (0,)), ((), ())), preferred_element_type=F32)


def registers(slab):
    return [slab[16 * j : 16 * j + 16] for j in range(NJ)]


def least(parts):
    parts = list(parts)
    while len(parts) > 1:
        parts = [jnp.minimum(parts[i], parts[i + 1]) for i in range(0, len(parts), 2)]
    m = parts[0].astype(F32)
    m = jnp.minimum(m[:8], m[8:])
    for s in (4, 2, 1):
        m = jnp.minimum(m, pltpu.roll(m, s, 0))
    return m


def step(v, m, c, cq, cm, q1, q1_low, q1_high):
    low = pltpu.roll(v[NJ - 1], 1, 0) + q1_low
    high = pltpu.roll(v[0], 15, 0) + q1_high
    w = []
    for j in range(NJ):
        if j == 0:
            sides = jnp.minimum(low, v[1] + q1)
        elif j == NJ - 1:
            sides = jnp.minimum(high, v[NJ - 2] + q1)
        else:
            sides = jnp.minimum(v[j - 1], v[j + 1]) + q1
        w.append(jnp.minimum(v[j], sides) + c[j])
    a = least([w[1], w[2], w[3], w[4], w[5], w[6], w[0], w[7]])
    whole = jnp.concatenate([m, m], axis=0).astype(BF16)
    return [jnp.minimum(w[j] - whole, cq[j]) for j in range(NJ)], jnp.minimum(a - m, cm)


def kernel(
    small_ref, large_ref, costs_ref, left_ref, right_ref,
    send_0, send_1, send_2, beyond_0, beyond_1, beyond_2,
    c_h, cq_h, cm_h, c_v, cq_v, cm_v, path_h, path_v, acc,
    out_h, in_h, out_v, in_v, send_h, recv_h, send_v, recv_v, send_b, recv_b,
):
    row, col = lax.axis_index("row"), lax.axis_index("col")
    rows, cols = lax.axis_size("row"), lax.axis_size("col")

    barrier = pltpu.get_barrier_semaphore()
    partners = [
        (col > 0, row, col - 1),
        (col < cols - 1, row, col + 1),
        (row > 0, row - 1, col),
        (row < rows - 1, row + 1, col),
    ]
    for there, r, c in partners:

        @pl.when(there)
        def _(r=r, c=c):
            pl.semaphore_signal(barrier, inc=1, device_id=(r, c), device_id_type=MESH)


    q1f = jnp.full((16, 128), small_ref[0].astype(F32))
    q2f = jnp.full((16, 128), large_ref[0].astype(F32))
    sub = lax.broadcasted_iota(jnp.int32, (16, 128), 0)
    q1, q2 = q1f.astype(BF16), q2f.astype(BF16)
    q1_low = jnp.where(sub == 0, FAR, q1f).astype(BF16)
    q1_high = jnp.where(sub == 15, FAR, q1f).astype(BF16)
    lane = lax.broadcasted_iota(jnp.int32, (16, 128), 1)
    after = [lane >= 32 * h for h in range(4)]
    r0 = lax.broadcasted_iota(jnp.int32, (D, D), 0)
    r1 = lax.broadcasted_iota(jnp.int32, (D, D), 1)
    perm = (r1 == (r0 % 16) * 8 + r0 // 16).astype(F32).astype(BF16)
    back = (r0 == (r1 % 16) * 8 + r1 // 16).astype(F32).astype(BF16)

    def keep(c_ref, cq_ref, cm_ref, n, slab):
        slab = slab.astype(BF16)
        cq = [c + q2 for c in registers(slab)]
        c_ref[n] = slab
        cq_ref[n] = jnp.concatenate(cq, axis=0)
        cm_ref[n] = least(cq)

    @pl.loop(0, TH)
    def _(y):
        acc[pl.ds(pl.multiple_of(y * PITCH, 8), TW), :] = costs_ref[y].astype(F32)

    @pl.loop(0, TW, unroll=16)
    def _(x):
        a = acc[pl.ds(x, TH, stride=PITCH), :].astype(BF16)
        keep(c_h, cq_h, cm_h, x, nt_dot(perm, jnp.concatenate([a] * 4, axis=0)))

    def columns():
        @pl.loop(0, TH, unroll=4)
        def _(y):
            keep(c_v, cq_v, cm_v, y, nt_dot(perm, costs_ref[y]))

    def h_copy(way):
        return pltpu.make_async_remote_copy(
            out_h.at[way], in_h.at[way], send_h.at[way], recv_h.at[way],
            device_id=(row, col + 1 - 2 * way), device_id_type=MESH,
        )

    def v_copy(way):
        return pltpu.make_async_remote_copy(
            out_v.at[way], in_v.at[way], send_v.at[way], recv_v.at[way],
            device_id=(row + 1 - 2 * way, col), device_id_type=MESH,
        )

    def arrived(way, at):
        @pl.when(at == 0)
        def _():
            in_h[way] = jnp.zeros((32, 128), BF16)

        @pl.when(at > 0)
        def _():
            h_copy(way).wait_recv()

        got = in_h[way].astype(F32)
        got = [got[:16], got[16:]]
        turned = [[v] + [pltpu.roll(v, 32 * k, 1) for k in (1, 2, 3)] for v in got]
        v = []
        for g in range(4):
            for i in range(2):
                u = turned[i][-g % 4]
                for h in range(1, 4):
                    u = jnp.where(after[h], turned[i][(h - g) % 4], u)
                v.append(u)
        return v

    def run_row(way, start, count, v, m):
        def body(t, carry):
            x = jnp.where(way == 0, start + t, TW - 1 - start - t)
            v, m = step(*carry, registers(c_h[x]), registers(cq_h[x]), cm_h[x], q1, q1_low, q1_high)
            path_h[way, x] = jnp.concatenate(v, axis=0)
            return v, m

        return lax.fori_loop(0, count, body, (v, m), unroll=32)

    def along_row(way):
        at = jnp.where(way == 0, col, cols - 1 - col)
        v = [a.astype(BF16) for a in arrived(way, at)]
        v, _ = run_row(way, 0, TW, v, least(v))

        @pl.when(at < cols - 1)
        def _():
            packed = []
            for i in range(2):
                u = v[i]
                for g in range(1, 4):
                    u = jnp.where(after[g], v[2 * g + i], u)
                packed.append(u)
            out_h[way] = jnp.concatenate(packed, axis=0)
            h_copy(way).start()

    def along_col(way):
        at = jnp.where(way == 0, row, rows - 1 - row)

        @pl.when(at == 0)
        def _():
            in_v[way] = jnp.zeros((D, 128), BF16)

        @pl.when(at > 0)
        def _():
            v_copy(way).wait_recv()

        v = [a.astype(BF16) for a in registers(in_v[way].astype(F32))]

        def body(t, carry):
            y = jnp.where(way == 0, t, TH - 1 - t)
            v, m = step(*carry, registers(c_v[y]), registers(cq_v[y]), cm_v[y], q1, q1_low, q1_high)
            path_v[way, y] = jnp.concatenate(v, axis=0)
            return v, m

        v, _ = lax.fori_loop(0, TH, body, (v, least(v)), unroll=8)

        @pl.when(at < rows - 1)
        def _():
            out_v[way] = jnp.concatenate(v, axis=0)
            v_copy(way).start()

    missing = sum(jnp.where(there, 0, 1) for there, _, _ in partners)
    pl.semaphore_wait(barrier, 4 - missing)

    near = jnp.minimum(col, cols - 1 - col)
    h_one = jnp.where(col * 2 < cols, 0, 1)
    v_near = jnp.minimum(row, rows - 1 - row)
    v_one = jnp.where(row * 2 < rows, 0, 1)
    before = jnp.minimum((near * 3) // 4, 4)
    until = before + ((cols - 2 - 2 * near) * 3) // 4

    def add_columns():
        @pl.loop(0, TH, unroll=2)
        def _(y):
            both = jnp.concatenate([path_v[0, y], path_v[1, y]], axis=0)
            both = nn_dot(jnp.concatenate([back, back], axis=1), both)
            acc[pl.ds(pl.multiple_of(y * PITCH, 8), TW), :] = jnp.transpose(both)

    def add_rows(way, start, count):
        @pl.loop(0, count, unroll=8)
        def _(n):
            g = start + n
            v = registers(path_h[way, 4 * g])
            for k in range(1, 4):
                v = [jnp.where(after[k], b, a) for a, b in zip(v, registers(path_h[way, 4 * g + k]))]
            v = jnp.transpose(nn_dot(back, jnp.concatenate(v, axis=0)))
            for k in range(4):
                at = pl.ds(4 * g + k, TH, stride=PITCH)
                acc[at, :] = acc[at, :] + v[TH * k : TH * (k + 1)]

    v_late = rows - 1 - v_near >= until

    @pl.loop(0, 9)
    def _(p):
        part, which = p // 3, p % 3
        slot = jnp.where(which == 0, v_near, rows - 1 - v_near)
        v_part = jnp.where(slot < before, 0, jnp.where(slot < until, 1, 2))

        @pl.when(p == jnp.where(near < 2, 3, 0))
        def _():
            columns()

        @pl.when(p == jnp.where(v_late, 8, 5))
        def _():
            add_columns()
            add_rows(h_one, 0, TW // 4)

        @pl.when(jnp.logical_and(which == 2, part < 2))
        def _():
            along_row(jnp.where(part == 0, h_one, 1 - h_one))

        @pl.when(jnp.logical_and(which < 2, v_part == part))
        def _():
            along_col(jnp.where(which == 0, v_one, 1 - v_one))

    CW = TW // 4
    last = 1 - h_one
    lane32 = lax.broadcasted_iota(jnp.int32, (CW, D), 1)
    blocks = ((send_0, beyond_0), (send_1, beyond_1), (send_2, beyond_2))

    def next_tile(q):
        return pltpu.make_async_remote_copy(
            blocks[q][0], blocks[q][1], send_b.at[q], recv_b.at[q],
            device_id=(row, col - 1), device_id_type=MESH,
        )

    def left_block(y, q):
        v = acc[pl.ds(pl.multiple_of(y * PITCH + q * CW, 8), CW), :] * (1.0 / 64.0)
        left_ref[y, q * CW : (q + 1) * CW] = v.astype(BF16)
        return v

    def send_block(n):
        for q in ((0,), (1, 3), (2,))[n]:
            add_rows(last, q * (CW // 4), CW // 4)

        @pl.loop(0, TH, unroll=4)
        def _(y):
            if n == 0:
                v = left_block(y, 0)
            elif n == 1:
                v = jnp.where(lane32 < 32, pltpu.roll(left_block(y, 3), 32, 1), left_block(y, 1))
            else:
                v = left_block(y, 2)
                v = jnp.where(lane32[:16] < 64, pltpu.roll(v[16:], 64, 1), v[:16])
            blocks[n][0][y] = v.astype(BF16)

        @pl.when(col > 0)
        def _():
            next_tile(n).start()

    def unfold(y, p):
        v = [beyond_0[y].astype(F32)]
        if p > 0:
            one = beyond_1[y].astype(F32)
            v.append(one)
        if p > 1:
            two = beyond_2[y].astype(F32)
            v += [two, pltpu.roll(two, 64, 1)]
        if p > 2:
            v.append(pltpu.roll(one, 96, 1))
        return v

    for n in range(3):
        send_block(n)

    @pl.when(col == cols - 1)
    def _():
        for _, b in blocks:
            b[...] = jnp.zeros(b.shape, BF16)

    for p in range(4):

        if p < 3:

            @pl.when(col < cols - 1)
            def _(p=p):
                next_tile(p).wait_recv()

        @pl.loop(0, TH, unroll=8)
        def _(y, p=p):
            v = [left_ref[y, p * CW :].astype(F32)] + unfold(y, p)
            v = jnp.concatenate(v, axis=0)
            for bit, size in ((64, 96), (32, 64), (16, 48), (8, 40)):
                d = lax.broadcasted_iota(jnp.int32, (size, D), 1)
                v = jnp.where((d & bit) != 0, v[bit : bit + size], v[:size])
            d = lax.broadcasted_iota(jnp.int32, (40, D), 1)
            for bit in (4, 2, 1):
                v = jnp.where((d & bit) != 0, pltpu.roll(v, 40 - bit, 0), v)
            right_ref[y, p * CW : (p + 1) * CW] = v[:CW].astype(BF16)

    for way in (0, 1):
        at_h = col if way == 0 else cols - 1 - col
        at_v = row if way == 0 else rows - 1 - row

        @pl.when(at_h < cols - 1)
        def _(way=way):
            h_copy(way).wait_send()

        @pl.when(at_v < rows - 1)
        def _(way=way):
            v_copy(way).wait_send()

    @pl.when(col > 0)
    def _():
        for q in range(3):
            next_tile(q).wait_send()


def put(left_ref, right_ref, left_out, right_out, sem):
    one = pltpu.make_async_copy(left_ref, left_out, sem.at[0])
    two = pltpu.make_async_copy(right_ref, right_out, sem.at[1])
    one.start()
    two.start()
    one.wait()
    two.wait()


def shards(costs, p_small, p_large):
    tile = jax.ShapeDtypeStruct(costs.shape, BF16)
    left, right = pl.pallas_call(
        kernel,
        out_shape=(pltpu.VMEM(costs.shape, BF16), pltpu.VMEM(costs.shape, BF16)),
        in_specs=[
            pl.BlockSpec(memory_space=pltpu.SMEM),
            pl.BlockSpec(memory_space=pltpu.SMEM),
            pl.BlockSpec(memory_space=pltpu.VMEM),
        ],
        out_specs=(pl.BlockSpec(memory_space=pltpu.VMEM), pl.BlockSpec(memory_space=pltpu.VMEM)),
        scratch_shapes=[
            *[pltpu.VMEM((TH, n, D), BF16) for n in (32, 32, 16)],
            *[pltpu.VMEM((TH, n, D), BF16) for n in (32, 32, 16)],
            pltpu.VMEM((TW, D, 128), BF16),
            pltpu.VMEM((TW, D, 128), BF16),
            pltpu.VMEM((TW, 8, 128), F32),
            pltpu.VMEM((TH, D, 128), BF16),
            pltpu.VMEM((TH, D, 128), BF16),
            pltpu.VMEM((TH, 8, 128), F32),
            pltpu.VMEM((2, TW, D, 128), BF16),
            pltpu.VMEM((2, TH, D, 128), BF16),
            pltpu.VMEM((TH * PITCH, D), F32),
            pltpu.VMEM((2, 32, 128), BF16),
            pltpu.VMEM((2, 32, 128), BF16),
            pltpu.VMEM((2, D, 128), BF16),
            pltpu.VMEM((2, D, 128), BF16),
            pltpu.SemaphoreType.DMA((2,)),
            pltpu.SemaphoreType.DMA((2,)),
            pltpu.SemaphoreType.DMA((2,)),
            pltpu.SemaphoreType.DMA((2,)),
            pltpu.SemaphoreType.DMA((3,)),
            pltpu.SemaphoreType.DMA((3,)),
        ],
        compiler_params=pltpu.CompilerParams(collective_id=0, has_side_effects=True, vmem_limit_bytes=48 << 20),
        name="sgm",
    )(p_small, p_large, costs)
    return pl.pallas_call(
        put,
        out_shape=(tile, tile),
        in_specs=[pl.BlockSpec(memory_space=pltpu.VMEM)] * 2,
        out_specs=(pl.BlockSpec(memory_space=pl.ANY), pl.BlockSpec(memory_space=pl.ANY)),
        scratch_shapes=[pltpu.SemaphoreType.DMA((2,))],
        compiler_params=pltpu.CompilerParams(vmem_limit_bytes=8 << 20),
        name="put",
    )(left, right)


def solution(mesh):
    placed = (P("row", "col", None), P(), P())
    return jax.shard_map(
        shards,
        mesh=mesh,
        in_specs=placed,
        out_specs=(P("row", "col", None), P("row", "col", None)),
        check_vma=False,
    )
```

```python
import jax
import jax.numpy as jnp
from jax import lax
from jax.experimental import pallas as pl
from jax.experimental.pallas import tpu as pltpu
from jax.sharding import PartitionSpec as P

MESH = pl.DeviceIdType.MESH
F32 = jnp.float32
BF16 = jnp.bfloat16
FAR = 1.0e9

TH, TW, D = 32, 128, 128
NJ = 8
PITCH = 136


def nt_dot(a, b):
    return lax.dot_general(a, b, (((1,), (1,)), ((), ())), preferred_element_type=F32)


def nn_dot(a, b):
    return lax.dot_general(a, b, (((1,), (0,)), ((), ())), preferred_element_type=F32)


def registers(slab):
    return [slab[16 * j : 16 * j + 16] for j in range(NJ)]


def least(parts):
    parts = list(parts)
    while len(parts) > 1:
        parts = [jnp.minimum(parts[i], parts[i + 1]) for i in range(0, len(parts), 2)]
    m = parts[0].astype(F32)
    m = jnp.minimum(m[:8], m[8:])
    for s in (4, 2, 1):
        m = jnp.minimum(m, pltpu.roll(m, s, 0))
    return m


def step(v, m, c, cq, cm, q1, q1_low, q1_high):
    low = pltpu.roll(v[NJ - 1], 1, 0) + q1_low
    high = pltpu.roll(v[0], 15, 0) + q1_high
    w = []
    for j in range(NJ):
        if j == 0:
            sides = jnp.minimum(low, v[1] + q1)
        elif j == NJ - 1:
            sides = jnp.minimum(high, v[NJ - 2] + q1)
        else:
            sides = jnp.minimum(v[j - 1], v[j + 1]) + q1
        w.append(jnp.minimum(v[j], sides) + c[j])
    a = least([w[1], w[2], w[3], w[4], w[5], w[6], w[0], w[7]])
    whole = jnp.concatenate([m, m], axis=0).astype(BF16)
    return [jnp.minimum(w[j] - whole, cq[j]) for j in range(NJ)], jnp.minimum(a - m, cm)


def kernel(
    small_ref, large_ref, costs_ref, left_ref, right_ref,
    send_0, send_1, send_2, beyond_0, beyond_1, beyond_2,
    c_h, cq_h, cm_h, c_v, cq_v, cm_v, path_h, path_v, acc,
    out_h, in_h, out_v, in_v, send_h, recv_h, send_v, recv_v, send_b, recv_b,
):
    row, col = lax.axis_index("row"), lax.axis_index("col")
    rows, cols = lax.axis_size("row"), lax.axis_size("col")

    barrier = pltpu.get_barrier_semaphore()
    partners = [
        (col > 0, row, col - 1),
        (col < cols - 1, row, col + 1),
        (row > 0, row - 1, col),
        (row < rows - 1, row + 1, col),
    ]
    for there, r, c in partners:

        @pl.when(there)
        def _(r=r, c=c):
            pl.semaphore_signal(barrier, inc=1, device_id=(r, c), device_id_type=MESH)


    q1f = jnp.full((16, 128), small_ref[0].astype(F32))
    q2f = jnp.full((16, 128), large_ref[0].astype(F32))
    sub = lax.broadcasted_iota(jnp.int32, (16, 128), 0)
    q1, q2 = q1f.astype(BF16), q2f.astype(BF16)
    q1_low = jnp.where(sub == 0, FAR, q1f).astype(BF16)
    q1_high = jnp.where(sub == 15, FAR, q1f).astype(BF16)
    lane = lax.broadcasted_iota(jnp.int32, (16, 128), 1)
    after = [lane >= 32 * h for h in range(4)]
    r0 = lax.broadcasted_iota(jnp.int32, (D, D), 0)
    r1 = lax.broadcasted_iota(jnp.int32, (D, D), 1)
    perm = (r1 == (r0 % 16) * 8 + r0 // 16).astype(F32).astype(BF16)
    back = (r0 == (r1 % 16) * 8 + r1 // 16).astype(F32).astype(BF16)

    def keep(c_ref, cq_ref, cm_ref, n, slab):
        slab = slab.astype(BF16)
        cq = [c + q2 for c in registers(slab)]
        c_ref[n] = slab
        cq_ref[n] = jnp.concatenate(cq, axis=0)
        cm_ref[n] = least(cq)

    @pl.loop(0, TH)
    def _(y):
        acc[pl.ds(pl.multiple_of(y * PITCH, 8), TW), :] = costs_ref[y].astype(F32)

    @pl.loop(0, TW, unroll=16)
    def _(x):
        a = acc[pl.ds(x, TH, stride=PITCH), :].astype(BF16)
        keep(c_h, cq_h, cm_h, x, nt_dot(perm, jnp.concatenate([a] * 4, axis=0)))

    def columns():
        @pl.loop(0, TH, unroll=4)
        def _(y):
            keep(c_v, cq_v, cm_v, y, nt_dot(perm, costs_ref[y]))

    def h_copy(way):
        return pltpu.make_async_remote_copy(
            out_h.at[way], in_h.at[way], send_h.at[way], recv_h.at[way],
            device_id=(row, col + 1 - 2 * way), device_id_type=MESH,
        )

    def v_copy(way):
        return pltpu.make_async_remote_copy(
            out_v.at[way], in_v.at[way], send_v.at[way], recv_v.at[way],
            device_id=(row + 1 - 2 * way, col), device_id_type=MESH,
        )

    def arrived(way, at):
        @pl.when(at == 0)
        def _():
            in_h[way] = jnp.zeros((32, 128), BF16)

        @pl.when(at > 0)
        def _():
            h_copy(way).wait_recv()

        got = in_h[way].astype(F32)
        got = [got[:16], got[16:]]
        turned = [[v] + [pltpu.roll(v, 32 * k, 1) for k in (1, 2, 3)] for v in got]
        v = []
        for g in range(4):
            for i in range(2):
                u = turned[i][-g % 4]
                for h in range(1, 4):
                    u = jnp.where(after[h], turned[i][(h - g) % 4], u)
                v.append(u)
        return v

    def run_row(way, start, count, v, m):
        def body(t, carry):
            x = jnp.where(way == 0, start + t, TW - 1 - start - t)
            v, m = step(*carry, registers(c_h[x]), registers(cq_h[x]), cm_h[x], q1, q1_low, q1_high)
            path_h[way, x] = jnp.concatenate(v, axis=0)
            return v, m

        return lax.fori_loop(0, count, body, (v, m), unroll=32)

    def along_row(way):
        at = jnp.where(way == 0, col, cols - 1 - col)
        v = [a.astype(BF16) for a in arrived(way, at)]
        v, _ = run_row(way, 0, TW, v, least(v))

        @pl.when(at < cols - 1)
        def _():
            packed = []
            for i in range(2):
                u = v[i]
                for g in range(1, 4):
                    u = jnp.where(after[g], v[2 * g + i], u)
                packed.append(u)
            out_h[way] = jnp.concatenate(packed, axis=0)
            h_copy(way).start()

    def along_col(way):
        at = jnp.where(way == 0, row, rows - 1 - row)

        @pl.when(at == 0)
        def _():
            in_v[way] = jnp.zeros((D, 128), BF16)

        @pl.when(at > 0)
        def _():
            v_copy(way).wait_recv()

        v = [a.astype(BF16) for a in registers(in_v[way].astype(F32))]

        def body(t, carry):
            y = jnp.where(way == 0, t, TH - 1 - t)
            v, m = step(*carry, registers(c_v[y]), registers(cq_v[y]), cm_v[y], q1, q1_low, q1_high)
            path_v[way, y] = jnp.concatenate(v, axis=0)
            return v, m

        v, _ = lax.fori_loop(0, TH, body, (v, least(v)), unroll=8)

        @pl.when(at < rows - 1)
        def _():
            out_v[way] = jnp.concatenate(v, axis=0)
            v_copy(way).start()

    missing = sum(jnp.where(there, 0, 1) for there, _, _ in partners)
    pl.semaphore_wait(barrier, 4 - missing)

    near = jnp.minimum(col, cols - 1 - col)
    h_one = jnp.where(col * 2 < cols, 0, 1)
    v_near = jnp.minimum(row, rows - 1 - row)
    v_one = jnp.where(row * 2 < rows, 0, 1)
    before = jnp.minimum((near * 3) // 4, 4)
    until = before + ((cols - 2 - 2 * near) * 3) // 4

    def add_columns():
        @pl.loop(0, TH, unroll=2)
        def _(y):
            both = jnp.concatenate([path_v[0, y], path_v[1, y]], axis=0)
            both = nn_dot(jnp.concatenate([back, back], axis=1), both)
            acc[pl.ds(pl.multiple_of(y * PITCH, 8), TW), :] = jnp.transpose(both)

    def add_rows(way, start, count):
        @pl.loop(0, count, unroll=8)
        def _(n):
            g = start + n
            v = registers(path_h[way, 4 * g])
            for k in range(1, 4):
                v = [jnp.where(after[k], b, a) for a, b in zip(v, registers(path_h[way, 4 * g + k]))]
            v = jnp.transpose(nn_dot(back, jnp.concatenate(v, axis=0)))
            for k in range(4):
                at = pl.ds(4 * g + k, TH, stride=PITCH)
                acc[at, :] = acc[at, :] + v[TH * k : TH * (k + 1)]

    v_late = rows - 1 - v_near >= until

    @pl.loop(0, 9)
    def _(p):
        part, which = p // 3, p % 3
        slot = jnp.where(which == 0, v_near, rows - 1 - v_near)
        v_part = jnp.where(slot < before, 0, jnp.where(slot < until, 1, 2))

        @pl.when(p == jnp.where(near < 2, 3, 0))
        def _():
            columns()

        @pl.when(p == jnp.where(v_late, 8, 5))
        def _():
            add_columns()
            add_rows(h_one, 0, TW // 4)

        @pl.when(jnp.logical_and(which == 2, part < 2))
        def _():
            along_row(jnp.where(part == 0, h_one, 1 - h_one))

        @pl.when(jnp.logical_and(which < 2, v_part == part))
        def _():
            along_col(jnp.where(which == 0, v_one, 1 - v_one))

    CW = TW // 4
    last = 1 - h_one
    lane32 = lax.broadcasted_iota(jnp.int32, (CW, D), 1)
    blocks = ((send_0, beyond_0), (send_1, beyond_1), (send_2, beyond_2))

    def next_tile(q):
        return pltpu.make_async_remote_copy(
            blocks[q][0], blocks[q][1], send_b.at[q], recv_b.at[q],
            device_id=(row, col - 1), device_id_type=MESH,
        )

    def left_block(y, q):
        v = acc[pl.ds(pl.multiple_of(y * PITCH + q * CW, 8), CW), :] * (1.0 / 64.0)
        left_ref[y, q * CW : (q + 1) * CW] = v.astype(BF16)
        return v

    def send_block(n):
        for q in ((0,), (1, 3), (2,))[n]:
            add_rows(last, q * (CW // 4), CW // 4)

        @pl.loop(0, TH, unroll=8)
        def _(y):
            if n == 0:
                v = left_block(y, 0)
            elif n == 1:
                v = jnp.where(lane32 < 32, pltpu.roll(left_block(y, 3), 32, 1), left_block(y, 1))
            else:
                v = left_block(y, 2)
                v = jnp.where(lane32[:16] < 64, pltpu.roll(v[16:], 64, 1), v[:16])
            blocks[n][0][y] = v.astype(BF16)

        @pl.when(col > 0)
        def _():
            next_tile(n).start()

    def unfold(y, p):
        v = [beyond_0[y].astype(F32)]
        if p > 0:
            one = beyond_1[y].astype(F32)
            v.append(one)
        if p > 1:
            two = beyond_2[y].astype(F32)
            v += [two, pltpu.roll(two, 64, 1)]
        if p > 2:
            v.append(pltpu.roll(one, 96, 1))
        return v

    for n in range(3):
        send_block(n)

    @pl.when(col == cols - 1)
    def _():
        for _, b in blocks:
            b[...] = jnp.zeros(b.shape, BF16)

    for p in range(4):

        if p < 3:

            @pl.when(col < cols - 1)
            def _(p=p):
                next_tile(p).wait_recv()

        @pl.loop(0, TH, unroll=16)
        def _(y, p=p):
            v = [left_ref[y, p * CW :].astype(F32)] + unfold(y, p)
            v = jnp.concatenate(v, axis=0)
            for bit, size in ((64, 96), (32, 64), (16, 48), (8, 40)):
                d = lax.broadcasted_iota(jnp.int32, (size, D), 1)
                v = jnp.where((d & bit) != 0, v[bit : bit + size], v[:size])
            d = lax.broadcasted_iota(jnp.int32, (40, D), 1)
            for bit in (4, 2, 1):
                v = jnp.where((d & bit) != 0, pltpu.roll(v, 40 - bit, 0), v)
            right_ref[y, p * CW : (p + 1) * CW] = v[:CW].astype(BF16)

    for way in (0, 1):
        at_h = col if way == 0 else cols - 1 - col
        at_v = row if way == 0 else rows - 1 - row

        @pl.when(at_h < cols - 1)
        def _(way=way):
            h_copy(way).wait_send()

        @pl.when(at_v < rows - 1)
        def _(way=way):
            v_copy(way).wait_send()

    @pl.when(col > 0)
    def _():
        for q in range(3):
            next_tile(q).wait_send()


def put(left_ref, right_ref, left_out, right_out, sem):
    one = pltpu.make_async_copy(left_ref, left_out, sem.at[0])
    two = pltpu.make_async_copy(right_ref, right_out, sem.at[1])
    one.start()
    two.start()
    one.wait()
    two.wait()


def shards(costs, p_small, p_large):
    tile = jax.ShapeDtypeStruct(costs.shape, BF16)
    left, right = pl.pallas_call(
        kernel,
        out_shape=(pltpu.VMEM(costs.shape, BF16), pltpu.VMEM(costs.shape, BF16)),
        in_specs=[
            pl.BlockSpec(memory_space=pltpu.SMEM),
            pl.BlockSpec(memory_space=pltpu.SMEM),
            pl.BlockSpec(memory_space=pltpu.VMEM),
        ],
        out_specs=(pl.BlockSpec(memory_space=pltpu.VMEM), pl.BlockSpec(memory_space=pltpu.VMEM)),
        scratch_shapes=[
            *[pltpu.VMEM((TH, n, D), BF16) for n in (32, 32, 16)],
            *[pltpu.VMEM((TH, n, D), BF16) for n in (32, 32, 16)],
            pltpu.VMEM((TW, D, 128), BF16),
            pltpu.VMEM((TW, D, 128), BF16),
            pltpu.VMEM((TW, 8, 128), F32),
            pltpu.VMEM((TH, D, 128), BF16),
            pltpu.VMEM((TH, D, 128), BF16),
            pltpu.VMEM((TH, 8, 128), F32),
            pltpu.VMEM((2, TW, D, 128), BF16),
            pltpu.VMEM((2, TH, D, 128), BF16),
            pltpu.VMEM((TH * PITCH, D), F32),
            pltpu.VMEM((2, 32, 128), BF16),
            pltpu.VMEM((2, 32, 128), BF16),
            pltpu.VMEM((2, D, 128), BF16),
            pltpu.VMEM((2, D, 128), BF16),
            pltpu.SemaphoreType.DMA((2,)),
            pltpu.SemaphoreType.DMA((2,)),
            pltpu.SemaphoreType.DMA((2,)),
            pltpu.SemaphoreType.DMA((2,)),
            pltpu.SemaphoreType.DMA((3,)),
            pltpu.SemaphoreType.DMA((3,)),
        ],
        compiler_params=pltpu.CompilerParams(collective_id=0, has_side_effects=True, vmem_limit_bytes=48 << 20),
        name="sgm",
    )(p_small, p_large, costs)
    return pl.pallas_call(
        put,
        out_shape=(tile, tile),
        in_specs=[pl.BlockSpec(memory_space=pltpu.VMEM)] * 2,
        out_specs=(pl.BlockSpec(memory_space=pl.ANY), pl.BlockSpec(memory_space=pl.ANY)),
        scratch_shapes=[pltpu.SemaphoreType.DMA((2,))],
        compiler_params=pltpu.CompilerParams(vmem_limit_bytes=8 << 20),
        name="put",
    )(left, right)


def solution(mesh):
    placed = (P("row", "col", None), P(), P())
    return jax.shard_map(
        shards,
        mesh=mesh,
        in_specs=placed,
        out_specs=(P("row", "col", None), P("row", "col", None)),
        check_vma=False,
    )
```

```python
import jax
import jax.numpy as jnp
from jax import lax
from jax.experimental import pallas as pl
from jax.experimental.pallas import tpu as pltpu
from jax.sharding import PartitionSpec as P

MESH = pl.DeviceIdType.MESH
F32 = jnp.float32
BF16 = jnp.bfloat16
FAR = 1.0e9

TH, TW, D = 32, 128, 128
NJ = 8
PITCH = 136


def nt_dot(a, b):
    return lax.dot_general(a, b, (((1,), (1,)), ((), ())), preferred_element_type=F32)


def nn_dot(a, b):
    return lax.dot_general(a, b, (((1,), (0,)), ((), ())), preferred_element_type=F32)


def registers(slab):
    return [slab[16 * j : 16 * j + 16] for j in range(NJ)]


def least(parts):
    parts = list(parts)
    while len(parts) > 1:
        parts = [jnp.minimum(parts[i], parts[i + 1]) for i in range(0, len(parts), 2)]
    m = parts[0].astype(F32)
    m = jnp.minimum(m[:8], m[8:])
    for s in (4, 2, 1):
        m = jnp.minimum(m, pltpu.roll(m, s, 0))
    return m


def step(v, m, c, cq, cm, q1, q1_low, q1_high):
    low = pltpu.roll(v[NJ - 1], 1, 0) + q1_low
    high = pltpu.roll(v[0], 15, 0) + q1_high
    w = []
    for j in range(NJ):
        if j == 0:
            sides = jnp.minimum(low, v[1] + q1)
        elif j == NJ - 1:
            sides = jnp.minimum(high, v[NJ - 2] + q1)
        else:
            sides = jnp.minimum(v[j - 1], v[j + 1]) + q1
        w.append(jnp.minimum(v[j], sides) + c[j])
    a = least([w[1], w[2], w[3], w[4], w[5], w[6], w[0], w[7]])
    whole = jnp.concatenate([m, m], axis=0).astype(BF16)
    return [jnp.minimum(w[j] - whole, cq[j]) for j in range(NJ)], jnp.minimum(a - m, cm)


def kernel(
    small_ref, large_ref, costs_ref, left_ref, right_ref,
    send_0, send_1, send_2, beyond_0, beyond_1, beyond_2,
    c_h, cq_h, cm_h, c_v, cq_v, cm_v, path_h, path_v, acc,
    out_h, in_h, out_v, in_v, send_h, recv_h, send_v, recv_v, send_b, recv_b,
):
    row, col = lax.axis_index("row"), lax.axis_index("col")
    rows, cols = lax.axis_size("row"), lax.axis_size("col")

    barrier = pltpu.get_barrier_semaphore()
    partners = [
        (col > 0, row, col - 1),
        (col < cols - 1, row, col + 1),
        (row > 0, row - 1, col),
        (row < rows - 1, row + 1, col),
    ]
    for there, r, c in partners:

        @pl.when(there)
        def _(r=r, c=c):
            pl.semaphore_signal(barrier, inc=1, device_id=(r, c), device_id_type=MESH)


    q1f = jnp.full((16, 128), small_ref[0].astype(F32))
    q2f = jnp.full((16, 128), large_ref[0].astype(F32))
    sub = lax.broadcasted_iota(jnp.int32, (16, 128), 0)
    q1, q2 = q1f.astype(BF16), q2f.astype(BF16)
    q1_low = jnp.where(sub == 0, FAR, q1f).astype(BF16)
    q1_high = jnp.where(sub == 15, FAR, q1f).astype(BF16)
    lane = lax.broadcasted_iota(jnp.int32, (16, 128), 1)
    after = [lane >= 32 * h for h in range(4)]
    r0 = lax.broadcasted_iota(jnp.int32, (D, D), 0)
    r1 = lax.broadcasted_iota(jnp.int32, (D, D), 1)
    perm = (r1 == (r0 % 16) * 8 + r0 // 16).astype(F32).astype(BF16)
    back = (r0 == (r1 % 16) * 8 + r1 // 16).astype(F32).astype(BF16)

    def keep(c_ref, cq_ref, cm_ref, n, slab):
        slab = slab.astype(BF16)
        cq = [c + q2 for c in registers(slab)]
        c_ref[n] = slab
        cq_ref[n] = jnp.concatenate(cq, axis=0)
        cm_ref[n] = least(cq)

    @pl.loop(0, TH)
    def _(y):
        acc[pl.ds(pl.multiple_of(y * PITCH, 8), TW), :] = costs_ref[y].astype(F32)

    @pl.loop(0, TW, unroll=16)
    def _(x):
        a = acc[pl.ds(x, TH, stride=PITCH), :].astype(BF16)
        keep(c_h, cq_h, cm_h, x, nt_dot(perm, jnp.concatenate([a] * 4, axis=0)))

    def columns():
        @pl.loop(0, TH, unroll=4)
        def _(y):
            keep(c_v, cq_v, cm_v, y, nt_dot(perm, costs_ref[y]))

    def h_copy(way):
        return pltpu.make_async_remote_copy(
            out_h.at[way], in_h.at[way], send_h.at[way], recv_h.at[way],
            device_id=(row, col + 1 - 2 * way), device_id_type=MESH,
        )

    def v_copy(way):
        return pltpu.make_async_remote_copy(
            out_v.at[way], in_v.at[way], send_v.at[way], recv_v.at[way],
            device_id=(row + 1 - 2 * way, col), device_id_type=MESH,
        )

    def arrived(way, at):
        @pl.when(at == 0)
        def _():
            in_h[way] = jnp.zeros((32, 128), BF16)

        @pl.when(at > 0)
        def _():
            h_copy(way).wait_recv()

        got = in_h[way].astype(F32)
        got = [got[:16], got[16:]]
        turned = [[v] + [pltpu.roll(v, 32 * k, 1) for k in (1, 2, 3)] for v in got]
        v = []
        for g in range(4):
            for i in range(2):
                u = turned[i][-g % 4]
                for h in range(1, 4):
                    u = jnp.where(after[h], turned[i][(h - g) % 4], u)
                v.append(u)
        return v

    def run_row(way, start, count, v, m):
        def body(t, carry):
            x = jnp.where(way == 0, start + t, TW - 1 - start - t)
            v, m = step(*carry, registers(c_h[x]), registers(cq_h[x]), cm_h[x], q1, q1_low, q1_high)
            path_h[way, x] = jnp.concatenate(v, axis=0)
            return v, m

        return lax.fori_loop(0, count, body, (v, m), unroll=32)

    def along_row(way):
        at = jnp.where(way == 0, col, cols - 1 - col)
        v = [a.astype(BF16) for a in arrived(way, at)]
        v, _ = run_row(way, 0, TW, v, least(v))

        @pl.when(at < cols - 1)
        def _():
            packed = []
            for i in range(2):
                u = v[i]
                for g in range(1, 4):
                    u = jnp.where(after[g], v[2 * g + i], u)
                packed.append(u)
            out_h[way] = jnp.concatenate(packed, axis=0)
            h_copy(way).start()

    def along_col(way):
        at = jnp.where(way == 0, row, rows - 1 - row)

        @pl.when(at == 0)
        def _():
            in_v[way] = jnp.zeros((D, 128), BF16)

        @pl.when(at > 0)
        def _():
            v_copy(way).wait_recv()

        v = [a.astype(BF16) for a in registers(in_v[way].astype(F32))]

        def body(t, carry):
            y = jnp.where(way == 0, t, TH - 1 - t)
            v, m = step(*carry, registers(c_v[y]), registers(cq_v[y]), cm_v[y], q1, q1_low, q1_high)
            path_v[way, y] = jnp.concatenate(v, axis=0)
            return v, m

        v, _ = lax.fori_loop(0, TH, body, (v, least(v)), unroll=8)

        @pl.when(at < rows - 1)
        def _():
            out_v[way] = jnp.concatenate(v, axis=0)
            v_copy(way).start()

    missing = sum(jnp.where(there, 0, 1) for there, _, _ in partners)
    pl.semaphore_wait(barrier, 4 - missing)

    near = jnp.minimum(col, cols - 1 - col)
    h_one = jnp.where(col * 2 < cols, 0, 1)
    v_near = jnp.minimum(row, rows - 1 - row)
    v_one = jnp.where(row * 2 < rows, 0, 1)
    before = jnp.minimum((near * 3) // 4, 4)
    until = before + ((cols - 2 - 2 * near) * 3) // 4

    def add_columns():
        @pl.loop(0, TH, unroll=2)
        def _(y):
            both = jnp.concatenate([path_v[0, y], path_v[1, y]], axis=0)
            both = nn_dot(jnp.concatenate([back, back], axis=1), both)
            acc[pl.ds(pl.multiple_of(y * PITCH, 8), TW), :] = jnp.transpose(both)

    def add_rows(way, start, count):
        @pl.loop(0, count, unroll=8)
        def _(n):
            g = start + n
            v = registers(path_h[way, 4 * g])
            for k in range(1, 4):
                v = [jnp.where(after[k], b, a) for a, b in zip(v, registers(path_h[way, 4 * g + k]))]
            v = jnp.transpose(nn_dot(back, jnp.concatenate(v, axis=0)))
            for k in range(4):
                at = pl.ds(4 * g + k, TH, stride=PITCH)
                acc[at, :] = acc[at, :] + v[TH * k : TH * (k + 1)]

    v_late = rows - 1 - v_near >= until

    @pl.loop(0, 9)
    def _(p):
        part, which = p // 3, p % 3
        slot = jnp.where(which == 0, v_near, rows - 1 - v_near)
        v_part = jnp.where(slot < before, 0, jnp.where(slot < until, 1, 2))

        @pl.when(p == jnp.where(near < 2, 3, 0))
        def _():
            columns()

        @pl.when(p == jnp.where(v_late, 8, 5))
        def _():
            add_columns()
            add_rows(h_one, 0, TW // 4)

        @pl.when(jnp.logical_and(which == 2, part < 2))
        def _():
            along_row(jnp.where(part == 0, h_one, 1 - h_one))

        @pl.when(jnp.logical_and(which < 2, v_part == part))
        def _():
            along_col(jnp.where(which == 0, v_one, 1 - v_one))

    CW = TW // 4
    last = 1 - h_one
    lane32 = lax.broadcasted_iota(jnp.int32, (CW, D), 1)
    blocks = ((send_0, beyond_0), (send_1, beyond_1), (send_2, beyond_2))

    def next_tile(q):
        return pltpu.make_async_remote_copy(
            blocks[q][0], blocks[q][1], send_b.at[q], recv_b.at[q],
            device_id=(row, col - 1), device_id_type=MESH,
        )

    def left_block(y, q):
        v = acc[pl.ds(pl.multiple_of(y * PITCH + q * CW, 8), CW), :] * (1.0 / 64.0)
        left_ref[y, q * CW : (q + 1) * CW] = v.astype(BF16)
        return v

    def send_block(n):
        for q in ((0,), (1, 3), (2,))[n]:
            add_rows(last, q * (CW // 4), CW // 4)

        @pl.loop(0, TH, unroll=8)
        def _(y):
            if n == 0:
                v = left_block(y, 0)
            elif n == 1:
                v = jnp.where(lane32 < 32, pltpu.roll(left_block(y, 3), 32, 1), left_block(y, 1))
            else:
                v = left_block(y, 2)
                v = jnp.where(lane32[:16] < 64, pltpu.roll(v[16:], 64, 1), v[:16])
            blocks[n][0][y] = v.astype(BF16)

        @pl.when(col > 0)
        def _():
            next_tile(n).start()

    def unfold(y, p):
        v = [beyond_0[y].astype(F32)]
        if p > 0:
            one = beyond_1[y].astype(F32)
            v.append(one)
        if p > 1:
            two = beyond_2[y].astype(F32)
            v += [two, pltpu.roll(two, 64, 1)]
        if p > 2:
            v.append(pltpu.roll(one, 96, 1))
        return v

    for n in range(3):
        send_block(n)

    @pl.when(col == cols - 1)
    def _():
        for _, b in blocks:
            b[...] = jnp.zeros(b.shape, BF16)

    for p in range(4):

        if p < 3:

            @pl.when(col < cols - 1)
            def _(p=p):
                next_tile(p).wait_recv()

        @pl.loop(0, TH, unroll=16)
        def _(y, p=p):
            v = [left_ref[y, p * CW :].astype(F32)] + unfold(y, p)
            v = jnp.concatenate(v, axis=0)
            for bit, size in ((64, 96), (32, 64), (16, 48), (8, 40)):
                d = lax.broadcasted_iota(jnp.int32, (size, D), 1)
                v = jnp.where((d & bit) != 0, v[bit : bit + size], v[:size])
            d = lax.broadcasted_iota(jnp.int32, (40, D), 1)
            for bit in (4, 2, 1):
                v = jnp.where((d & bit) != 0, pltpu.roll(v, 40 - bit, 0), v)
            right_ref[y, p * CW : (p + 1) * CW] = v[:CW].astype(BF16)

    for way in (0, 1):
        at_h = col if way == 0 else cols - 1 - col
        at_v = row if way == 0 else rows - 1 - row

        @pl.when(at_h < cols - 1)
        def _(way=way):
            h_copy(way).wait_send()

        @pl.when(at_v < rows - 1)
        def _(way=way):
            v_copy(way).wait_send()

    @pl.when(col > 0)
    def _():
        for q in range(3):
            next_tile(q).wait_send()


def put(left_ref, right_ref, left_out, right_out, sem):
    one = pltpu.make_async_copy(left_ref, left_out, sem.at[0])
    two = pltpu.make_async_copy(right_ref, right_out, sem.at[1])
    one.start()
    two.start()
    one.wait()
    two.wait()


def shards(costs, p_small, p_large):
    tile = jax.ShapeDtypeStruct(costs.shape, BF16)
    left, right = pl.pallas_call(
        kernel,
        out_shape=(pltpu.VMEM(costs.shape, BF16), pltpu.VMEM(costs.shape, BF16)),
        in_specs=[
            pl.BlockSpec(memory_space=pltpu.SMEM),
            pl.BlockSpec(memory_space=pltpu.SMEM),
            pl.BlockSpec(memory_space=pltpu.VMEM),
        ],
        out_specs=(pl.BlockSpec(memory_space=pltpu.VMEM), pl.BlockSpec(memory_space=pltpu.VMEM)),
        scratch_shapes=[
            *[pltpu.VMEM((TH, n, D), BF16) for n in (32, 32, 16)],
            *[pltpu.VMEM((TH, n, D), BF16) for n in (32, 32, 16)],
            pltpu.VMEM((TW, D, 128), BF16),
            pltpu.VMEM((TW, D, 128), BF16),
            pltpu.VMEM((TW, 8, 128), F32),
            pltpu.VMEM((TH, D, 128), BF16),
            pltpu.VMEM((TH, D, 128), BF16),
            pltpu.VMEM((TH, 8, 128), F32),
            pltpu.VMEM((2, TW, D, 128), BF16),
            pltpu.VMEM((2, TH, D, 128), BF16),
            pltpu.VMEM(((TH + 1) * PITCH, D), F32),
            pltpu.VMEM((2, 32, 128), BF16),
            pltpu.VMEM((2, 32, 128), BF16),
            pltpu.VMEM((2, D, 128), BF16),
            pltpu.VMEM((2, D, 128), BF16),
            pltpu.SemaphoreType.DMA((2,)),
            pltpu.SemaphoreType.DMA((2,)),
            pltpu.SemaphoreType.DMA((2,)),
            pltpu.SemaphoreType.DMA((2,)),
            pltpu.SemaphoreType.DMA((3,)),
            pltpu.SemaphoreType.DMA((3,)),
        ],
        compiler_params=pltpu.CompilerParams(collective_id=0, has_side_effects=True, vmem_limit_bytes=48 << 20),
        name="sgm",
    )(p_small, p_large, costs)
    return pl.pallas_call(
        put,
        out_shape=(tile, tile),
        in_specs=[pl.BlockSpec(memory_space=pltpu.VMEM)] * 2,
        out_specs=(pl.BlockSpec(memory_space=pl.ANY), pl.BlockSpec(memory_space=pl.ANY)),
        scratch_shapes=[pltpu.SemaphoreType.DMA((2,))],
        compiler_params=pltpu.CompilerParams(vmem_limit_bytes=8 << 20),
        name="put",
    )(left, right)


def solution(mesh):
    placed = (P("row", "col", None), P(), P())
    return jax.shard_map(
        shards,
        mesh=mesh,
        in_specs=placed,
        out_specs=(P("row", "col", None), P("row", "col", None)),
        check_vma=False,
    )
```
